32 devices in a mesh: dp: 4 (over z), ctx: 8 (over y, x, core).
Axes of the slice: x: 2, y: 2, z: 4, core: 2. Of those that a mesh axis runs over, the one named last changes fastest.
Arguments:
- tokens: bfloat16 [4, 1024, 8192], P('dp', 'ctx'), may hold values from -6 to 6
- w_down: bfloat16 [8192, 512], P(('dp', 'ctx')), may hold values from -0.0625 to 0.0625
- w_up: bfloat16 [512, 1024], replicated, may hold values from -0.25 to 0.25
- queries: bfloat16 [4, 1024, 4096], P('dp', 'ctx'), may hold values from -70 to 70, as said below
- block_order: int32 [4, 16], P('dp', 'ctx'), may hold values from 0 to 15, each once within a row
Outputs:
- attended: bfloat16 [4, 1024, 4096], P('dp', 'ctx')
The draws below stay inside these ranges and needn't reach their ends.
Inputs may be any that keep to these rules, and one draw needn't show every extreme that they name: `queries`: query entries.
All inputs are finite; a program needn't handle non-finite values.
Results may differ from the reference program's by a relative error of at most 0.014.
The reference program's roundings to bfloat16 on the way count: a program that leaves them out, or rounds other values in their place, can miss the bound.
Values may be sent and summed in bfloat16 or wider, within the bound.
A program may use at most 64 MiB of HBM per device.

```python
import jax
import jax.numpy as jnp
from jax import lax

D = 8192
R = 512
QH = 32
KVH = 4
HD = 128
HALF = 64
SEQ = 1024
N_DP = 4
N_CTX = 8


def draw_queries(key, part):
    shape = (N_DP, SEQ, QH * HD)
    return jnp.clip(jax.random.normal(key, shape, jnp.float32), -6.0, 6.0).astype(jnp.bfloat16)


def shard_levels(key, extent, pieces, least, high):
    loudness = 1.0
    for dim, parts in pieces:
        heights = jax.random.uniform(jax.random.fold_in(jax.random.fold_in(key, 6), dim), (parts,), jnp.float32, least / len(pieces), high / len(pieces))
        loudness = loudness * jnp.repeat(jnp.exp(heights), extent[dim] // parts).reshape((-1,) + (1,) * (len(extent) - 1 - dim))
    return loudness


def gaussian(rng, dims, width, most, cuts=(), kind=jnp.bfloat16):
    gain = shard_levels(rng, dims, cuts, -0.22, 0.18) if cuts else 1.0
    array = jax.random.normal(rng, dims, jnp.float32) * width * gain
    return jnp.minimum(jnp.maximum(array, -most), most).astype(kind)


def setup_inputs(seed: int = 0) -> dict:
    seeds = jax.random.split(jax.random.key(seed), 6)
    tokens = gaussian(seeds[0], (N_DP, SEQ, D), 1.0, 6.0, ((0, 4), (1, 8)))
    w_down = gaussian(seeds[1], (D, R), D ** -0.5, 0.0625, ((0, 32),))
    w_up = gaussian(seeds[2], (R, 2 * KVH * HD), R ** -0.5, 0.25)
    queries = draw_queries(jax.random.fold_in(seeds[5], 71), 0)
    block_order = jax.vmap(lambda own: jax.random.permutation(own, 2 * N_CTX))(jax.random.split(seeds[4], N_DP)).reshape((N_DP, 2 * N_CTX)).astype(jnp.int32)
    return dict(tokens=tokens, w_down=w_down, w_up=w_up, queries=queries, block_order=block_order)


def one_sequence(tokens_one, queries_one, order_one, w_down, w_up):
    latent = jnp.dot(tokens_one, w_down, preferred_element_type=jnp.float32).astype(jnp.bfloat16)
    kv_rows = jnp.dot(latent, w_up, preferred_element_type=jnp.float32).astype(jnp.bfloat16)
    row_ids = jnp.arange(SEQ, dtype=jnp.int32)
    position = jnp.take(order_one, row_ids // HALF).astype(jnp.int32) * HALF + row_ids % HALF
    key_heads = kv_rows[:, :KVH * HD].reshape(SEQ, KVH, HD).transpose(1, 0, 2)
    value_heads = kv_rows[:, KVH * HD:].reshape(SEQ, KVH, HD).transpose(1, 0, 2)
    query_heads = queries_one.reshape(SEQ, QH, HD).transpose(1, 0, 2)
    allowed = position[None, :] <= position[:, None]
    group = QH // KVH
    score_scale = HD ** -0.5

    def head(index):
        kv_index = index // group
        scores = jnp.dot(query_heads[index], key_heads[kv_index].T, preferred_element_type=jnp.float32) * score_scale
        scores = jnp.where(allowed, scores, -1e30)
        largest = jnp.max(scores, axis=1)
        expo = jnp.where(allowed, jnp.exp(scores - largest[:, None]), 0.0)
        total = jnp.sum(expo, axis=1)
        summed = jnp.dot(expo.astype(jnp.bfloat16), value_heads[kv_index], preferred_element_type=jnp.float32)
        return summed / total[:, None]

    outputs = lax.map(head, jnp.arange(QH, dtype=jnp.int32))
    return outputs.transpose(1, 0, 2).reshape(SEQ, QH * HD).astype(jnp.bfloat16)


def reference(tokens, w_down, w_up, queries, block_order):
    def single(args):
        return one_sequence(args[0], args[1], args[2], w_down, w_up)
    return lax.map(single, (tokens, queries, block_order))
```

```python
import functools
import math

import jax
import jax.numpy as jnp
from jax import lax
from jax.experimental import pallas as pl
from jax.experimental.pallas import tpu as pltpu
from jax.sharding import PartitionSpec as P

QH = 32
KVH = 4
HD = 128
MESH = pl.DeviceIdType.MESH


def attention_kernel(order_ref, pos_ref, latent_ref, w_up_ref, q_ref, out_ref, keys, values, hidden):
    rows = q_ref.shape[1]
    count = latent_ref.shape[0]
    half = rows // 2
    tile = math.gcd(count, 256)

    @pl.loop(0, count // tile)
    def _(i):
        part = pl.ds(pl.multiple_of(i * tile, tile), tile)
        both = jnp.dot(
            latent_ref[part, :], w_up_ref[...], preferred_element_type=jnp.float32
        ).astype(jnp.bfloat16)
        for g in range(KVH):
            keys[g, part, 0:HD] = both[:, g * HD : (g + 1) * HD]
            values[g, part, 0:HD] = both[:, (KVH + g) * HD : (KVH + g + 1) * HD]
            values[g, part, HD : 2 * HD] = jnp.ones((tile, HD), jnp.bfloat16)
        dims = lax.broadcasted_iota(jnp.int32, (rows, tile), 0)
        first, step = dims // half, dims % half
        block = jnp.where(first == 0, order_ref[0, 0], order_ref[0, 1])
        place = pos_ref[0:1, part]
        inside = jnp.logical_and(place // half == block, jnp.logical_and(step == place % half, step > 0))
        later = jnp.logical_and(place // half > block, step == 0)
        marks = jnp.where(jnp.logical_or(inside, later), 1.0, 0.0).T.astype(jnp.bfloat16)
        for g in range(KVH):
            keys[g, part, HD : 2 * HD] = marks

    ids = lax.broadcasted_iota(jnp.int32, (rows, HD), 0)
    dims = lax.broadcasted_iota(jnp.int32, (rows, HD), 1)
    own = ids // half == dims // half
    blocked = jnp.logical_or(dims % half == 0, dims % half > ids % half)
    hidden[...] = jnp.where(jnp.logical_and(own, blocked), -1e30, 0.0).astype(jnp.bfloat16)
    scale = HD ** (-0.5) * math.log2(math.e)
    heads = 8
    group = QH // KVH

    def cols(first, width):
        return pl.ds(pl.multiple_of(first * HD, HD), width * HD)

    def score(i):
        queries = jnp.concatenate(
            [
                jnp.concatenate([q_ref[0, :, cols(i * heads + k, 1)], hidden[...]], axis=1)
                for k in range(heads)
            ],
            axis=0,
        )
        return lax.dot_general(
            queries,
            keys[i * heads // group],
            (((1,), (1,)), ((), ())),
            preferred_element_type=jnp.float32,
        )

    def weigh(i, scores):
        parts = []
        for first in range(0, heads * rows, strip):
            kept = scores[first : first + strip]
            largest = jnp.max(kept, axis=1, keepdims=True)
            parts.append(jnp.exp2((kept - largest) * scale).astype(jnp.bfloat16))
        summed = jnp.dot(
            jnp.concatenate(parts, axis=0),
            values[i * heads // group],
            preferred_element_type=jnp.float32,
        )
        summed = (summed[:, 0:HD] / summed[:, HD : 2 * HD]).astype(jnp.bfloat16)
        for k in range(heads):
            out_ref[0, :, cols(i * heads + k, 1)] = summed[k * rows : (k + 1) * rows]

    sets = QH // heads
    together = sets if count <= 1024 else 1
    strip = 16

    @pl.loop(0, sets // together)
    def _(i):
        scores = score(i * together)
        for k in range(together):
            ahead = score(i * together + k + 1) if k + 1 < together else None
            weigh(i * together + k, scores)
            scores = ahead


def attend(block_order, positions, latent, w_up, queries):
    count = latent.shape[0]
    rows = queries.shape[1]
    vmem = pl.BlockSpec(memory_space=pltpu.VMEM)
    return pl.pallas_call(
        attention_kernel,
        out_shape=jax.ShapeDtypeStruct(queries.shape, jnp.bfloat16),
        in_specs=[pl.BlockSpec(memory_space=pltpu.SMEM), vmem, vmem, vmem, vmem],
        out_specs=vmem,
        scratch_shapes=[
            pltpu.VMEM((KVH, count, 2 * HD), jnp.bfloat16),
            pltpu.VMEM((KVH, count, 2 * HD), jnp.bfloat16),
            pltpu.VMEM((rows, HD), jnp.bfloat16),
        ],
        compiler_params=pltpu.CompilerParams(vmem_limit_bytes=60 * 2**20),
        name="attention",
    )(block_order, positions, latent, w_up, queries)


PLACES = "sxyd"
HELPED = 2
MIRROR = {0: 3, 1: 2, 2: 1, 3: 0}
BY_Z = ((2, 0),)
IN_PLANE = ((3, 0), (3, 1), (1, 1))
END_STEPS = [
    ('tokens',), ('send', 0, 8), ('w', 0, 'x', 0, None), ('w', 0, 'y', 0, None), ('w', 1, 's', 0, None),
    ('w', 0, 'x', 1, None), ('w', 0, 'y', 1, None), ('w', 1, 's', 1, None), ('w', 0, 'd', 0, 0),
    ('w', 0, 'd', 0, 1), ('w', 1, 'x', 0, None), ('w', 1, 'y', 0, None), ('w', 0, 'd', 1, 0), ('w', 0, 'd', 1, 1),
    ('w', 3, 's', 0, None), ('w', 1, 'x', 1, None), ('w', 1, 'y', 1, None), ('w', 1, 'd', 0, 0),
    ('w', 1, 'd', 0, 1), ('w', 3, 'x', 0, None), ('w', 3, 'y', 0, None), ('w', 3, 's', 1, None),
    ('w', 1, 'd', 1, 0), ('w', 1, 'd', 1, 1), ('w', 3, 'd', 0, 0), ('w', 3, 'd', 0, 1), ('swap', 0),
    ('w', 3, 'x', 1, None), ('w', 3, 'y', 1, None), ('sum', 0), ('l', 'm', 0), ('w', 3, 'd', 1, 0),
    ('w', 3, 'd', 1, 1), ('swap', 1), ('l', 'xl', 0), ('l', 'yh', 0), ('l', 'xh', 0), ('l', 'yl', 0), ('sum', 1),
    ('l', 'mx', 0), ('l', 'my', 0), ('l', 'm', 1), ('l', 'dl', 0), ('l', 'dh', 0), ('l', 'xl', 1), ('l', 'yh', 1),
    ('l', 'mdl', 0), ('l', 'mdh', 0), ('l', 'xh', 1), ('l', 'yl', 1), ('l', 'mx', 1), ('l', 'my', 1),
    ('l', 'dl', 1), ('l', 'dh', 1), ('l', 'mdl', 1), ('l', 'mdh', 1),
]
INNER_STEPS = [
    ('tokens',), ('w', 0, 's', 0, None), ('w', 1, 'x', 0, None), ('w', 1, 'y', 0, None), ('w', 2, 's', 0, None),
    ('w', 0, 's', 1, None), ('w', 1, 'x', 1, None), ('w', 1, 'y', 1, None), ('w', 2, 's', 1, None),
    ('w', 0, 'x', 0, None), ('w', 0, 'y', 0, None), ('w', 3, 's', 0, None), ('w', 1, 'd', 0, 0),
    ('w', 2, 'x', 0, 1), ('w', 1, 'd', 0, 1), ('w', 2, 'y', 0, 1), ('w', 2, 'x', 0, 0), ('w', 2, 'y', 0, 0),
    ('w', 0, 'x', 1, None), ('w', 0, 'y', 1, None), ('w', 3, 's', 1, None), ('w', 1, 'd', 1, 0),
    ('w', 1, 'd', 1, 1), ('w', 2, 'd', 0, 0), ('w', 2, 'd', 0, 1), ('hswap', 0), ('w', 2, 'x', 1, None),
    ('w', 2, 'y', 1, None), ('w', 0, 'd', 0, 0), ('w', 2, 'd', 1, 0), ('part', 0), ('w', 0, 'd', 0, 1),
    ('w', 2, 'd', 1, 1), ('hswap', 1), ('w', 3, 'x', 0, None), ('w', 3, 'y', 0, None), ('w', 0, 'd', 1, 0),
    ('w', 3, 'd', 0, 0), ('part', 1), ('w', 0, 'd', 1, 1), ('w', 3, 'd', 0, 1), ('swap', 0), ('w', 3, 'x', 1, None),
    ('w', 3, 'y', 1, None), ('w', 3, 'd', 1, 0), ('sum', 0), ('w', 3, 'd', 1, 1), ('swap', 1), ('l', 'm', 0),
    ('l', 'xl', 0), ('l', 'yh', 0), ('sum', 1), ('l', 'xh', 0), ('l', 'yl', 0), ('l', 'm', 1), ('l', 'mx', 0),
    ('l', 'my', 0), ('l', 'dl', 0), ('l', 'dh', 0), ('l', 'xl', 1), ('l', 'yh', 1), ('l', 'mdl', 0),
    ('l', 'mdh', 0), ('l', 'xh', 1), ('l', 'yl', 1), ('l', 'mx', 1), ('l', 'my', 1), ('l', 'dl', 1), ('l', 'dh', 1),
    ('l', 'mdl', 1), ('l', 'mdh', 1),
]


def route(end, piece):
    r, place, g, h = piece
    sends = []

    def to(link, r, place, h):
        sends.append((link, (r, place, g, h)))

    if place == "s":
        split = 0 if not end and (r, g) in BY_Z else None
        if end and r == 0:
            to("in", 0, "s", None)
        if not end and r == 1:
            to("in", 2, "s", None)
        if not end and r not in (0, HELPED):
            to("out", r, "s", None)
        to("x", r, "x", split)
        to("y", r, "y", split)
        if not end and r == 0:
            to("in", 3, "s", None)
    elif place in "xy":
        if r == (0 if end else 1) or (end and (r, g) in IN_PLANE):
            to(*(("y", r, "d", 0) if place == "x" else ("x", r, "d", 1)))
        if end and r == 0 and (0, g) in BY_Z:
            to("in", 0, place, 1)
        if not end and r == 0 and (3, g) in BY_Z and (h == 1 or (0, g) not in BY_Z):
            to("in", 3, place, 1)
        if not end and r == 1 and (2, g) in BY_Z:
            to("in", 2, place, 1)
    elif end:
        if r == 0:
            to("in", 0, "d", h)
    else:
        if r not in (0, HELPED) and (r, g) not in IN_PLANE:
            to("out", r, "d", h)
        if r in (0, 1):
            to("in", MIRROR[r], "d", h)
    return sends


def pieces(end, r, place, g):
    if place == "d" or (place in "xy" and not end and (r, g) in BY_Z):
        return 2
    return 1


def latent_kernel(
    order_ref, tokens_ref, w_ref, latent_ref, pos_ref,
    tok, helped, w, acc, extra, share, extra_share, partial, ready, mine, gathered, pos_mine, pos_all,
    load_sem, own_sem, tok_send, tok_recv, help_send, help_recv, w_send, w_recv,
    pos_send, pos_recv, sum_send, sum_recv, lat_send, lat_recv, store_sem,
):
    plane = 8
    z, ctx = lax.axis_index("dp"), lax.axis_index("ctx")
    core, x, y = ctx % 2, ctx // 2 % 2, ctx // 4
    mate = ctx + 1 - 2 * core
    x_dev, y_dev = ctx + 2 - 4 * x, ctx + 4 - 8 * y
    d_dev = (1 - y) * 4 + (1 - x) * 2 + core
    far = z // 2
    up = 1 - 2 * far
    rows, depth, width = tokens_ref.shape[1], w_ref.shape[0], w_ref.shape[1]
    groups = 2
    columns_each = width // groups
    half = depth // 2
    chip_rows = 2 * rows

    def feature(slot, side):
        r, bx, by = slot // 4, slot % 2, slot // 2 % 2
        chip = (y + by - 2 * y * by) * 2 + x + bx - 2 * x * bx
        layer = far * 3 + up * r
        return pl.ds(pl.multiple_of(((layer * 4 + chip) * 2 + side) * depth, depth), depth)

    def load(slot):
        return pltpu.make_async_copy(
            tokens_ref.at[0, :, feature(slot, core)], tok.at[slot, pl.ds(0, rows), :], load_sem.at[slot]
        )

    def swap(slot):
        return pltpu.make_async_remote_copy(
            tokens_ref.at[0, :, feature(slot, 1 - core)], tok.at[slot, pl.ds(rows, rows), :],
            tok_send.at[slot], tok_recv.at[slot], device_id=(z, mate), device_id_type=MESH,
        )

    def slot_of(r, place):
        return r * 4 + PLACES.index(place)

    def lines(h):
        return slice(None) if h is None else pl.ds(h * half, half)

    def group_columns(g):
        return pl.ds(g * columns_each, columns_each)

    barrier = pltpu.get_barrier_semaphore()
    for d in range(1, plane):
        pl.semaphore_signal(barrier, inc=1, device_id=(z, (ctx + d) % plane), device_id_type=MESH)

    half_rows = rows // 2
    ids = lax.broadcasted_iota(jnp.int32, (8, rows), 1)
    pos_mine[...] = jnp.where(ids < half_rows, order_ref[0, 0], order_ref[0, 1]) * half_rows + ids % half_rows

    def pos_slot(device):
        return pos_all.at[:, pl.ds(pl.multiple_of(device * rows, rows), rows)]

    def pos_copy(d):
        return pltpu.make_async_remote_copy(
            pos_mine, pos_slot(ctx), pos_send.at[d], pos_recv.at[ctx],
            device_id=(z, (ctx + d) % plane), device_id_type=MESH,
        )

    def program(end):
        own_r = 0 if end else 1
        own = slot_of(own_r, "s")
        devices = {"x": (z, x_dev), "y": (z, y_dev), "in": (z + up, ctx), "out": (z - up, ctx)}
        if end:
            greeted = [(z + up, ctx), (z + up, mate)]
        else:
            greeted = [(z - up, ctx), (z - up, mate), (z + up, ctx)]
        for device in greeted:
            pl.semaphore_signal(barrier, inc=1, device_id=device, device_id_type=MESH)
        own_loads = [
            pltpu.make_async_copy(w_ref.at[:, group_columns(g)], w.at[g, own], own_sem.at[g]) for g in range(groups)
        ]
        for copy in own_loads:
            copy.start()
        pl.semaphore_wait(barrier, plane - 1 + len(greeted))

        sent = []

        def start(copy):
            copy.start()
            sent.append(copy)

        def forward(piece):
            for link, (r, place, g, h) in route(end, piece):
                target = w.at[g, slot_of(r, place), lines(h), :]
                if piece[:2] == (own_r, "s"):
                    source = w_ref.at[lines(h), group_columns(g)]
                else:
                    source = w.at[g, slot_of(*piece[:2]), lines(h), :]
                start(pltpu.make_async_remote_copy(
                    source, target, w_send.at[len(sent)],
                    w_recv.at[g, slot_of(r, place), 1 if h == 1 else 0],
                    device_id=devices[link], device_id_type=MESH,
                ))

        def arrived(target, sem):
            pltpu.make_async_remote_copy(
                target, target, w_send.at[0], sem, device_id=(z, mate), device_id_type=MESH
            ).wait_recv()

        for g in range(groups):
            forward((own_r, "s", g, None))

        count = 12 if end else 16

        def used(i):
            return i + (i // (HELPED * 4)) * 4 if end else i

        def start_tokens(i, unused):
            swap(used(i)).start()
            load(used(i)).start()
            return unused

        lax.fori_loop(0, count, start_tokens, 0)

        for d in range(1, plane):
            pos_copy(d).start()
        pos_all[:, pl.ds(pl.multiple_of(ctx * rows, rows), rows)] = pos_mine[...]

        def help_copy(i):
            place, other = i % 4, i // 4
            side = core + other - 2 * core * other
            return pltpu.make_async_remote_copy(
                tokens_ref.at[0, :, feature(HELPED * 4 + place, side)],
                helped.at[place, pl.ds(other * rows, rows), :],
                help_send.at[i], help_recv.at[i],
                device_id=(z + up, ctx if other == 0 else mate), device_id_type=MESH,
            )

        got, waiting, state = {}, [], {"tokens": False, "helped": False}

        def multiply(slot, g):
            acc[g] += jnp.dot(tok[slot], w[g, slot], preferred_element_type=jnp.float32)

        def w_arrival(r, place, g, h):
            slot = slot_of(r, place)
            arrived(w.at[g, slot, lines(h), :], w_recv.at[g, slot, 1 if h == 1 else 0])
            forward((r, place, g, h))
            got[slot, g] = got.get((slot, g), 0) + 1
            if got[slot, g] == pieces(end, r, place, g):
                if state["tokens"]:
                    multiply(slot, g)
                else:
                    waiting.append((slot, g))

        def tokens_arrival():
            def wait_tokens(i, unused):
                load(used(i)).wait()
                swap(used(i)).wait()
                return unused

            lax.fori_loop(0, count, wait_tokens, 0)
            for g in range(groups):
                own_loads[g].wait()
                acc[g] = jnp.dot(tok[own], w[g, own], preferred_element_type=jnp.float32)
            state["tokens"] = True
            for slot, g in waiting:
                multiply(slot, g)

        def help_send_some(first, last):
            for i in range(first, last):
                start(help_copy(i))

        def exchange(source, target, index):
            return pltpu.make_async_remote_copy(
                source, target, sum_send.at[index], sum_recv.at[index], device_id=(z, mate), device_id_type=MESH
            )

        def swap_sum(g):
            return exchange(acc.at[g, pl.ds(rows, rows), :], share.at[g], g)

        def swap_extra(g):
            return exchange(extra.at[g, pl.ds(rows, rows), :], extra_share.at[g], groups + g)

        def send_partial(g):
            return pltpu.make_async_remote_copy(
                ready.at[g], partial.at[g], sum_send.at[2 * groups + g], sum_recv.at[2 * groups + g],
                device_id=(z - up, ctx), device_id_type=MESH,
            )

        def start_swap(g):
            start(swap_sum(g))

        def start_extra(g):
            if not state["helped"]:
                state["helped"] = True
                for i in range(8):
                    target = helped.at[i % 4, pl.ds(i // 4 * rows, rows), :]
                    arrived(target, help_recv.at[i])
            total = None
            for place in range(4):
                term = jnp.dot(helped[place], w[g, HELPED * 4 + place], preferred_element_type=jnp.float32)
                total = term if total is None else total + term
            extra[g] = total
            start(swap_extra(g))

        def finish_extra(g):
            swap_extra(g).wait_recv()
            ready[g] = extra[g, 0:rows, :] + extra_share[g]
            start(send_partial(g))

        part = rows // 2
        stores = []
        sends = {g: 0 for g in range(groups)}

        def block(g, device, first=0, size=rows):
            return gathered.at[g, pl.ds(pl.multiple_of(device * rows + first, part), size), :]

        def lat_send_to(g, source, target, recv, device):
            start(pltpu.make_async_remote_copy(
                source, target, lat_send.at[g, sends[g]], lat_recv.at[g, recv],
                device_id=(z, device), device_id_type=MESH,
            ))
            sends[g] += 1

        def store(g, source, device):
            copy = pltpu.make_async_copy(
                source, latent_ref.at[pl.ds(pl.multiple_of(device * rows, rows), rows), group_columns(g)],
                store_sem.at[len(stores)],
            )
            copy.start()
            stores.append(copy)

        def partner(device):
            return device + 1 - 2 * core

        def finish_sum(g):
            swap_sum(g).wait_recv()
            total = acc[g, 0:rows, :] + share[g]
            if end:
                send_partial(g).wait_recv()
                total = total + partial[g]
            mine[g] = total.astype(jnp.bfloat16)
            low, high = pl.ds(0, part), pl.ds(part, part)
            lat_send_to(g, mine.at[g, low, :], block(g, ctx, 0, part), 0, x_dev)
            lat_send_to(g, mine.at[g, high, :], block(g, ctx, part, part), 1, y_dev)
            lat_send_to(g, mine.at[g, high, :], block(g, ctx, part, part), 2, x_dev)
            lat_send_to(g, mine.at[g, low, :], block(g, ctx, 0, part), 3, y_dev)
            lat_send_to(g, mine.at[g], block(g, ctx), 4, mate)
            store(g, mine.at[g], ctx)

        def lat_arrival(code, g):
            def got_block(target, recv):
                arrived(target, lat_recv.at[g, recv])

            def pass_on(target, recv, device):
                lat_send_to(g, target, target, recv, device)

            if code == "xl":
                got_block(block(g, x_dev, 0, part), 0)
                pass_on(block(g, x_dev, 0, part), 5, y_dev)
            elif code == "yh":
                got_block(block(g, y_dev, part, part), 1)
                pass_on(block(g, y_dev, part, part), 6, x_dev)
            elif code == "xh":
                got_block(block(g, x_dev, part, part), 2)
                pass_on(block(g, x_dev), 7, mate)
                store(g, block(g, x_dev), x_dev)
            elif code == "yl":
                got_block(block(g, y_dev, 0, part), 3)
                pass_on(block(g, y_dev), 8, mate)
                store(g, block(g, y_dev), y_dev)
            elif code == "m":
                got_block(block(g, mate), 4)
                store(g, block(g, mate), mate)
            elif code == "dl":
                got_block(block(g, d_dev, 0, part), 5)
                pass_on(block(g, d_dev, 0, part), 9, mate)
            elif code == "dh":
                got_block(block(g, d_dev, part, part), 6)
                pass_on(block(g, d_dev, part, part), 10, mate)
                store(g, block(g, d_dev), d_dev)
            elif code == "mx":
                got_block(block(g, partner(x_dev)), 7)
                store(g, block(g, partner(x_dev)), partner(x_dev))
            elif code == "my":
                got_block(block(g, partner(y_dev)), 8)
                store(g, block(g, partner(y_dev)), partner(y_dev))
            elif code == "mdl":
                got_block(block(g, partner(d_dev), 0, part), 9)
            else:
                got_block(block(g, partner(d_dev), part, part), 10)
                store(g, block(g, partner(d_dev)), partner(d_dev))

        steps = dict(
            w=w_arrival, tokens=tokens_arrival, send=help_send_some, swap=start_swap, sum=finish_sum,
            hswap=start_extra, part=finish_extra, l=lat_arrival,
        )
        for kind, *where in END_STEPS if end else INNER_STEPS:
            steps[kind](*where)

        for d in range(1, plane):
            pos_copy(d).wait_send()
            sender = (ctx + d) % plane
            arrived(pos_slot(sender), pos_recv.at[sender])
        pos_store = pltpu.make_async_copy(pos_all, pos_ref, store_sem.at[len(stores)])
        pos_store.start()
        for copy in sent:
            copy.wait_send()
        for copy in stores:
            copy.wait()
        pos_store.wait()

    outer = jnp.logical_or(z == 0, z == 3)
    pl.when(outer)(lambda: program(True))
    pl.when(jnp.logical_not(outer))(lambda: program(False))


def gather_latent(tokens, w_down, block_order):
    rows = tokens.shape[1]
    depth, width = w_down.shape
    each = width // 2
    dma = pltpu.SemaphoreType.DMA
    whole = pl.BlockSpec(memory_space=pltpu.HBM)
    return pl.pallas_call(
        latent_kernel,
        out_shape=[
            jax.ShapeDtypeStruct((8 * rows, width), jnp.bfloat16),
            jax.ShapeDtypeStruct((8, 8 * rows), jnp.int32),
        ],
        in_specs=[pl.BlockSpec(memory_space=pltpu.SMEM), whole, whole],
        out_specs=[whole, whole],
        scratch_shapes=[
            pltpu.VMEM((16, 2 * rows, depth), jnp.bfloat16),
            pltpu.VMEM((4, 2 * rows, depth), jnp.bfloat16),
            pltpu.VMEM((2, 16, depth, each), jnp.bfloat16),
            pltpu.VMEM((2, 2 * rows, each), jnp.float32),
            pltpu.VMEM((2, 2 * rows, each), jnp.float32),
            pltpu.VMEM((2, rows, each), jnp.float32),
            pltpu.VMEM((2, rows, each), jnp.float32),
            pltpu.VMEM((2, rows, each), jnp.float32),
            pltpu.VMEM((2, rows, each), jnp.float32),
            pltpu.VMEM((2, rows, each), jnp.bfloat16),
            pltpu.VMEM((2, 8 * rows, each), jnp.bfloat16),
            pltpu.VMEM((8, rows), jnp.int32),
            pltpu.VMEM((8, 8 * rows), jnp.int32),
            dma((16,)),
            dma((2,)),
            dma((16,)),
            dma((16,)),
            dma((8,)),
            dma((8,)),
            dma((160,)),
            dma((2, 16, 2)),
            dma((8,)),
            dma((8,)),
            dma((6,)),
            dma((6,)),
            dma((2, 12)),
            dma((2, 11)),
            dma((20,)),
        ],
        compiler_params=pltpu.CompilerParams(
            collective_id=0, has_side_effects=True, vmem_limit_bytes=60 * 2**20
        ),
        name="latent",
    )(block_order, tokens, w_down)


def per_device(layers, plane, tokens, w_down, w_up, queries, block_order):
    local_rows = tokens.shape[1]
    half_rows = local_rows // 2
    if plane == 8 and layers == 4:
        latent, positions = gather_latent(tokens, w_down, block_order)
        return attend(block_order, positions, latent, w_up, queries)
    summed = jnp.dot(
        tokens[0],
        lax.all_gather(w_down, ("dp", "ctx"), axis=0, tiled=True),
        preferred_element_type=jnp.float32,
    )
    latent = lax.all_gather(summed.astype(jnp.bfloat16), "ctx", axis=0, tiled=True)
    order = lax.all_gather(block_order, "ctx", axis=1, tiled=True)
    positions = jnp.repeat(order, half_rows, axis=1) * half_rows + jnp.tile(
        jnp.arange(half_rows, dtype=jnp.int32), order.shape[1]
    )
    return attend(block_order, positions, latent, w_up, queries)


def solution(mesh):
    placed = (
        P("dp", "ctx", None),
        P(("dp", "ctx"), None),
        P(),
        P("dp", "ctx", None),
        P("dp", "ctx"),
    )
    sizes = mesh.shape["dp"], mesh.shape["ctx"]
    return jax.shard_map(
        functools.partial(per_device, *sizes), mesh=mesh, in_specs=placed, out_specs=P("dp", "ctx", None), check_vma=False
    )
```

```python
import functools
import math

import jax
import jax.numpy as jnp
from jax import lax
from jax.experimental import pallas as pl
from jax.experimental.pallas import tpu as pltpu
from jax.sharding import PartitionSpec as P

QH = 32
KVH = 4
HD = 128
MESH = pl.DeviceIdType.MESH


def attention_kernel(order_ref, pos_ref, latent_ref, w_up_ref, q_ref, out_ref, keys, values, hidden):
    rows = q_ref.shape[1]
    count = latent_ref.shape[0]
    half = rows // 2
    tile = math.gcd(count, 256)

    @pl.loop(0, count // tile)
    def _(i):
        part = pl.ds(pl.multiple_of(i * tile, tile), tile)
        both = jnp.dot(
            latent_ref[part, :], w_up_ref[...], preferred_element_type=jnp.float32
        ).astype(jnp.bfloat16)
        for g in range(KVH):
            keys[g, part, 0:HD] = both[:, g * HD : (g + 1) * HD]
            values[g, part, 0:HD] = both[:, (KVH + g) * HD : (KVH + g + 1) * HD]
            values[g, part, HD : 2 * HD] = jnp.ones((tile, HD), jnp.bfloat16)
        dims = lax.broadcasted_iota(jnp.int32, (rows, tile), 0)
        first, step = dims // half, dims % half
        block = jnp.where(first == 0, order_ref[0, 0], order_ref[0, 1])
        place = pos_ref[0:1, part]
        inside = jnp.logical_and(place // half == block, jnp.logical_and(step == place % half, step > 0))
        later = jnp.logical_and(place // half > block, step == 0)
        marks = jnp.where(jnp.logical_or(inside, later), 1.0, 0.0).T.astype(jnp.bfloat16)
        for g in range(KVH):
            keys[g, part, HD : 2 * HD] = marks

    ids = lax.broadcasted_iota(jnp.int32, (rows, HD), 0)
    dims = lax.broadcasted_iota(jnp.int32, (rows, HD), 1)
    own = ids // half == dims // half
    blocked = jnp.logical_or(dims % half == 0, dims % half > ids % half)
    hidden[...] = jnp.where(jnp.logical_and(own, blocked), -1e30, 0.0).astype(jnp.bfloat16)
    scale = HD ** (-0.5) * math.log2(math.e)
    heads = 8
    group = QH // KVH

    def cols(first, width):
        return pl.ds(pl.multiple_of(first * HD, HD), width * HD)

    def score(i):
        queries = jnp.concatenate(
            [
                jnp.concatenate([q_ref[0, :, cols(i * heads + k, 1)], hidden[...]], axis=1)
                for k in range(heads)
            ],
            axis=0,
        )
        return lax.dot_general(
            queries,
            keys[i * heads // group],
            (((1,), (1,)), ((), ())),
            preferred_element_type=jnp.float32,
        )

    def weigh(i, scores):
        parts = []
        for first in range(0, heads * rows, strip):
            kept = scores[first : first + strip]
            largest = jnp.max(kept, axis=1, keepdims=True)
            parts.append(jnp.exp2((kept - largest) * scale).astype(jnp.bfloat16))
        summed = jnp.dot(
            jnp.concatenate(parts, axis=0),
            values[i * heads // group],
            preferred_element_type=jnp.float32,
        )
        summed = (summed[:, 0:HD] / summed[:, HD : 2 * HD]).astype(jnp.bfloat16)
        for k in range(heads):
            out_ref[0, :, cols(i * heads + k, 1)] = summed[k * rows : (k + 1) * rows]

    sets = QH // heads
    together = sets if count <= 1024 else 1
    strip = 16

    @pl.loop(0, sets // together)
    def _(i):
        scores = score(i * together)
        for k in range(together):
            ahead = score(i * together + k + 1) if k + 1 < together else None
            weigh(i * together + k, scores)
            scores = ahead


def attend(block_order, positions, latent, w_up, queries):
    count = latent.shape[0]
    rows = queries.shape[1]
    vmem = pl.BlockSpec(memory_space=pltpu.VMEM)
    return pl.pallas_call(
        attention_kernel,
        out_shape=jax.ShapeDtypeStruct(queries.shape, jnp.bfloat16),
        in_specs=[pl.BlockSpec(memory_space=pltpu.SMEM), vmem, vmem, vmem, vmem],
        out_specs=vmem,
        scratch_shapes=[
            pltpu.VMEM((KVH, count, 2 * HD), jnp.bfloat16),
            pltpu.VMEM((KVH, count, 2 * HD), jnp.bfloat16),
            pltpu.VMEM((rows, HD), jnp.bfloat16),
        ],
        compiler_params=pltpu.CompilerParams(vmem_limit_bytes=60 * 2**20),
        name="attention",
    )(block_order, positions, latent, w_up, queries)


PLACES = "sxyd"
HELPED = 2
MIRROR = {0: 3, 1: 2, 2: 1, 3: 0}
BY_Z = ((2, 0),)
IN_PLANE = ((3, 0), (3, 1), (1, 1))
END_STEPS = [
    ('tokens',), ('send', 0, 8), ('w', 0, 'x', 0, None), ('w', 0, 'y', 0, None), ('w', 1, 's', 0, None),
    ('w', 0, 'x', 1, None), ('w', 0, 'y', 1, None), ('w', 1, 's', 1, None), ('w', 0, 'd', 0, 0),
    ('w', 0, 'd', 0, 1), ('w', 1, 'x', 0, None), ('w', 1, 'y', 0, None), ('w', 0, 'd', 1, 0), ('w', 0, 'd', 1, 1),
    ('w', 3, 's', 0, None), ('w', 1, 'x', 1, None), ('w', 1, 'y', 1, None), ('w', 1, 'd', 0, 0),
    ('w', 1, 'd', 0, 1), ('w', 3, 'x', 0, None), ('w', 3, 'y', 0, None), ('w', 3, 's', 1, None),
    ('w', 1, 'd', 1, 0), ('w', 1, 'd', 1, 1), ('w', 3, 'd', 0, 0), ('w', 3, 'd', 0, 1), ('swap', 0),
    ('w', 3, 'x', 1, None), ('w', 3, 'y', 1, None), ('sum', 0), ('w', 3, 'd', 1, 0), ('w', 3, 'd', 1, 1),
    ('swap', 1), ('sum', 1),
]
INNER_STEPS = [
    ('tokens',), ('w', 0, 's', 0, None), ('w', 1, 'x', 0, None), ('w', 1, 'y', 0, None), ('w', 2, 's', 0, None),
    ('w', 0, 's', 1, None), ('w', 1, 'x', 1, None), ('w', 1, 'y', 1, None), ('w', 2, 's', 1, None),
    ('w', 0, 'x', 0, None), ('w', 0, 'y', 0, None), ('w', 3, 's', 0, None), ('w', 1, 'd', 0, 0),
    ('w', 2, 'x', 0, 1), ('w', 1, 'd', 0, 1), ('w', 2, 'y', 0, 1), ('w', 2, 'x', 0, 0), ('w', 2, 'y', 0, 0),
    ('w', 0, 'x', 1, None), ('w', 0, 'y', 1, None), ('w', 3, 's', 1, None), ('w', 1, 'd', 1, 0),
    ('w', 1, 'd', 1, 1), ('w', 2, 'd', 0, 0), ('w', 2, 'd', 0, 1), ('hswap', 0), ('w', 2, 'x', 1, None),
    ('w', 2, 'y', 1, None), ('w', 0, 'd', 0, 0), ('w', 2, 'd', 1, 0), ('part', 0), ('w', 0, 'd', 0, 1),
    ('w', 2, 'd', 1, 1), ('hswap', 1), ('w', 3, 'x', 0, None), ('w', 3, 'y', 0, None), ('w', 0, 'd', 1, 0),
    ('w', 3, 'd', 0, 0), ('part', 1), ('w', 0, 'd', 1, 1), ('w', 3, 'd', 0, 1), ('swap', 0), ('w', 3, 'x', 1, None),
    ('w', 3, 'y', 1, None), ('w', 3, 'd', 1, 0), ('sum', 0), ('w', 3, 'd', 1, 1), ('swap', 1), ('sum', 1),
]
TAIL = [
    ([("xl", 0), ("yh", 0), ("xh", 0), ("yl", 0), ("m", 0), ("m", 1)],
     {2: [("dl", 0), ("dh", 0)], 5: [("xl", 1), ("yh", 1)], 8: [("xh", 1), ("yl", 1)]}),
    ([("mx", 0), ("mx", 1)], {3: [("dl", 1), ("dh", 1)]}),
    ([("my", 0), ("my", 1)], {}),
    ([("md", 0), ("md", 1)], {}),
]


def route(end, piece):
    r, place, g, h = piece
    sends = []

    def to(link, r, place, h):
        sends.append((link, (r, place, g, h)))

    if place == "s":
        split = 0 if not end and (r, g) in BY_Z else None
        if end and r == 0:
            to("in", 0, "s", None)
        if not end and r == 1:
            to("in", 2, "s", None)
        if not end and r not in (0, HELPED):
            to("out", r, "s", None)
        to("x", r, "x", split)
        to("y", r, "y", split)
        if not end and r == 0:
            to("in", 3, "s", None)
    elif place in "xy":
        if r == (0 if end else 1) or (end and (r, g) in IN_PLANE):
            to(*(("y", r, "d", 0) if place == "x" else ("x", r, "d", 1)))
        if end and r == 0 and (0, g) in BY_Z:
            to("in", 0, place, 1)
        if not end and r == 0 and (3, g) in BY_Z and (h == 1 or (0, g) not in BY_Z):
            to("in", 3, place, 1)
        if not end and r == 1 and (2, g) in BY_Z:
            to("in", 2, place, 1)
    elif end:
        if r == 0:
            to("in", 0, "d", h)
    else:
        if r not in (0, HELPED) and (r, g) not in IN_PLANE:
            to("out", r, "d", h)
        if r in (0, 1):
            to("in", MIRROR[r], "d", h)
    return sends


def pieces(end, r, place, g):
    if place == "d" or (place in "xy" and not end and (r, g) in BY_Z):
        return 2
    return 1


def layer_kernel(
    order_ref, tokens_ref, w_ref, w_up_ref, q_ref, out_ref,
    tok, helped, w, acc, extra, share, extra_share, partial, ready, mine, gathered, pos_mine, pos_all,
    w_up, q_all, q_cat, keys, values, weighed, highest, staged,
    load_sem, own_sem, tok_send, tok_recv, help_send, help_recv, w_send, w_recv,
    pos_send, pos_recv, sum_send, sum_recv, lat_send, lat_recv, late_sem, out_sem,
):
    plane = 8
    z, ctx = lax.axis_index("dp"), lax.axis_index("ctx")
    core, x, y = ctx % 2, ctx // 2 % 2, ctx // 4
    mate = ctx + 1 - 2 * core
    x_dev, y_dev = ctx + 2 - 4 * x, ctx + 4 - 8 * y
    d_dev = (1 - y) * 4 + (1 - x) * 2 + core
    far = z // 2
    up = 1 - 2 * far
    rows, depth, width = tokens_ref.shape[1], w_ref.shape[0], w_ref.shape[1]
    groups = 2
    columns_each = width // groups
    half = depth // 2
    chip_rows = 2 * rows

    def feature(slot, side):
        r, bx, by = slot // 4, slot % 2, slot // 2 % 2
        chip = (y + by - 2 * y * by) * 2 + x + bx - 2 * x * bx
        layer = far * 3 + up * r
        return pl.ds(pl.multiple_of(((layer * 4 + chip) * 2 + side) * depth, depth), depth)

    def load(slot):
        return pltpu.make_async_copy(
            tokens_ref.at[0, :, feature(slot, core)], tok.at[slot, pl.ds(0, rows), :], load_sem.at[slot]
        )

    def swap(slot):
        return pltpu.make_async_remote_copy(
            tokens_ref.at[0, :, feature(slot, 1 - core)], tok.at[slot, pl.ds(rows, rows), :],
            tok_send.at[slot], tok_recv.at[slot], device_id=(z, mate), device_id_type=MESH,
        )

    def slot_of(r, place):
        return r * 4 + PLACES.index(place)

    def lines(h):
        return slice(None) if h is None else slice(h * half, h * half + half)

    def group_columns(g):
        return pl.ds(g * columns_each, columns_each)

    barrier = pltpu.get_barrier_semaphore()
    for d in range(1, plane):
        pl.semaphore_signal(barrier, inc=1, device_id=(z, (ctx + d) % plane), device_id_type=MESH)

    half_rows = rows // 2
    ids = lax.broadcasted_iota(jnp.int32, (8, rows), 1)
    pos_mine[...] = jnp.where(ids < half_rows, order_ref[0, 0], order_ref[0, 1]) * half_rows + ids % half_rows

    def pos_slot(device):
        return pos_all.at[:, pl.ds(pl.multiple_of(device * rows, rows), rows)]

    def pos_copy(d):
        return pltpu.make_async_remote_copy(
            pos_mine, pos_slot(ctx), pos_send.at[d], pos_recv.at[ctx],
            device_id=(z, (ctx + d) % plane), device_id_type=MESH,
        )

    def arrived(target, sem):
        pltpu.make_async_remote_copy(
            target, target, w_send.at[0], sem, device_id=(z, mate), device_id_type=MESH
        ).wait_recv()

    def departed(source, sem):
        pltpu.make_async_remote_copy(
            source, source, sem, pos_recv.at[0], device_id=(z, mate), device_id_type=MESH
        ).wait_send()

    part = rows // 2

    def block(g, device, first=0, size=rows):
        return gathered.at[g, pl.ds(pl.multiple_of(device * rows + first, part), size), :]

    def lat_copy(g, index, source, target, device):
        return pltpu.make_async_remote_copy(
            source, target, lat_send.at[g, index], lat_recv.at[g, index],
            device_id=(z, device), device_id_type=MESH,
        )

    late_loads = [
        pltpu.make_async_copy(w_up_ref, w_up, late_sem.at[0]),
        pltpu.make_async_copy(q_ref.at[0], q_all, late_sem.at[1]),
    ]

    def prepare_queries():
        late_loads[1].wait()
        ids = lax.broadcasted_iota(jnp.int32, (rows, HD), 0)
        dims = lax.broadcasted_iota(jnp.int32, (rows, HD), 1)
        own = ids // half_rows == dims // half_rows
        blocked = jnp.logical_or(dims % half_rows == 0, dims % half_rows > ids % half_rows)
        hidden = jnp.where(jnp.logical_and(own, blocked), -1e30, 0.0).astype(jnp.bfloat16)
        for head in range(QH):
            own_rows = pl.ds(head % share_heads * rows, rows)
            q_cat[head // share_heads, own_rows, 0:HD] = q_all[:, head * HD : (head + 1) * HD]
            q_cat[head // share_heads, own_rows, HD : 2 * HD] = hidden
        late_loads[0].wait()

    share_heads = QH // KVH

    def program(end):
        own_r = 0 if end else 1
        own = slot_of(own_r, "s")
        devices = {"x": (z, x_dev), "y": (z, y_dev), "in": (z + up, ctx), "out": (z - up, ctx)}
        if end:
            greeted = [(z + up, ctx), (z + up, mate)]
        else:
            greeted = [(z - up, ctx), (z - up, mate), (z + up, ctx)]
        for device in greeted:
            pl.semaphore_signal(barrier, inc=1, device_id=device, device_id_type=MESH)
        own_loads = [
            pltpu.make_async_copy(w_ref.at[:, group_columns(g)], w.at[g, own], own_sem.at[g]) for g in range(groups)
        ]
        for copy in own_loads:
            copy.start()
        pl.semaphore_wait(barrier, plane - 1 + len(greeted))

        sent = []

        def start(copy, *like):
            copy.start()
            sent.append(like)

        def forward(piece):
            for link, (r, place, g, h) in route(end, piece):
                at = (g, slot_of(r, place), lines(h), slice(None))
                target = w.at[at]
                if piece[:2] == (own_r, "s"):
                    source = w_ref.at[lines(h), group_columns(g)]
                else:
                    source = w.at[g, slot_of(*piece[:2]), lines(h), :]
                start(pltpu.make_async_remote_copy(
                    source, target, w_send.at[len(sent)], w_recv.at[g, slot_of(r, place), 1 if h == 1 else 0],
                    device_id=devices[link], device_id_type=MESH,
                ), w, at, w_send, len(sent))

        for g in range(groups):
            forward((own_r, "s", g, None))

        count = 12 if end else 16

        def used(i):
            return i + (i // (HELPED * 4)) * 4 if end else i

        def start_tokens(i, unused):
            swap(used(i)).start()
            load(used(i)).start()
            return unused

        lax.fori_loop(0, count, start_tokens, 0)

        for copy in late_loads:
            copy.start()
        for d in range(1, plane):
            pos_copy(d).start()
        pos_all[:, pl.ds(pl.multiple_of(ctx * rows, rows), rows)] = pos_mine[...]

        prepare_queries()

        def help_copy(i):
            place, other = i % 4, i // 4
            side = core + other - 2 * core * other
            return pltpu.make_async_remote_copy(
                tokens_ref.at[0, :, feature(HELPED * 4 + place, side)],
                helped.at[place, pl.ds(other * rows, rows), :],
                help_send.at[i], help_recv.at[i],
                device_id=(z + up, ctx if other == 0 else mate), device_id_type=MESH,
            )

        got, waiting, state = {}, [], {"tokens": False, "helped": False}

        def multiply(slot, g):
            acc[g] += jnp.dot(tok[slot], w[g, slot], preferred_element_type=jnp.float32)

        def w_arrival(r, place, g, h):
            slot = slot_of(r, place)
            arrived(w.at[g, slot, lines(h), :], w_recv.at[g, slot, 1 if h == 1 else 0])
            forward((r, place, g, h))
            got[slot, g] = got.get((slot, g), 0) + 1
            if got[slot, g] == pieces(end, r, place, g):
                if state["tokens"]:
                    multiply(slot, g)
                else:
                    waiting.append((slot, g))

        def tokens_arrival():
            def wait_tokens(i, unused):
                load(used(i)).wait()
                swap(used(i)).wait()
                return unused

            lax.fori_loop(0, count, wait_tokens, 0)
            for g in range(groups):
                own_loads[g].wait()
                acc[g] = jnp.dot(tok[own], w[g, own], preferred_element_type=jnp.float32)
            state["tokens"] = True
            for slot, g in waiting:
                multiply(slot, g)

        def help_send_some(first, last):
            for i in range(first, last):
                start(help_copy(i), helped, (i % 4, slice(i // 4 * rows, i // 4 * rows + rows)), help_send, i)

        def exchange(source, target, index):
            return pltpu.make_async_remote_copy(
                source, target, sum_send.at[index], sum_recv.at[index], device_id=(z, mate), device_id_type=MESH
            )

        def swap_sum(g):
            return exchange(acc.at[g, pl.ds(rows, rows), :], share.at[g], g)

        def swap_extra(g):
            return exchange(extra.at[g, pl.ds(rows, rows), :], extra_share.at[g], groups + g)

        def send_partial(g):
            return pltpu.make_async_remote_copy(
                ready.at[g], partial.at[g], sum_send.at[2 * groups + g], sum_recv.at[2 * groups + g],
                device_id=(z - up, ctx), device_id_type=MESH,
            )

        def start_swap(g):
            start(swap_sum(g), share, g, sum_send, g)

        def start_extra(g):
            if not state["helped"]:
                state["helped"] = True
                for i in range(8):
                    target = helped.at[i % 4, pl.ds(i // 4 * rows, rows), :]
                    arrived(target, help_recv.at[i])
            total = None
            for place in range(4):
                term = jnp.dot(helped[place], w[g, HELPED * 4 + place], preferred_element_type=jnp.float32)
                total = term if total is None else total + term
            extra[g] = total
            start(swap_extra(g), extra_share, g, sum_send, groups + g)

        def finish_extra(g):
            swap_extra(g).wait_recv()
            ready[g] = extra[g, 0:rows, :] + extra_share[g]
            start(send_partial(g), partial, g, sum_send, 2 * groups + g)

        def finish_sum(g):
            swap_sum(g).wait_recv()
            total = acc[g, 0:rows, :] + share[g]
            if end:
                send_partial(g).wait_recv()
                total = total + partial[g]
            mine[g] = total.astype(jnp.bfloat16)
            low, high = pl.ds(0, part), pl.ds(part, part)
            lat_copy(g, 0, mine.at[g, low, :], block(g, ctx, 0, part), x_dev).start()
            lat_copy(g, 1, mine.at[g, high, :], block(g, ctx, part, part), y_dev).start()
            lat_copy(g, 2, mine.at[g, high, :], block(g, ctx, part, part), x_dev).start()
            lat_copy(g, 3, mine.at[g, low, :], block(g, ctx, 0, part), y_dev).start()
            lat_copy(g, 4, mine.at[g], block(g, ctx), mate).start()
            gathered[g, pl.ds(pl.multiple_of(ctx * rows, rows), rows), :] = mine[g]

        steps = dict(
            w=w_arrival, tokens=tokens_arrival, send=help_send_some, swap=start_swap, sum=finish_sum,
            hswap=start_extra, part=finish_extra,
        )
        for kind, *where in END_STEPS if end else INNER_STEPS:
            steps[kind](*where)
        return sent

    outer = jnp.logical_or(z == 0, z == 3)
    drains = {}

    def run(end):
        drains[end] = program(end)

    pl.when(outer)(lambda: run(True))
    pl.when(jnp.logical_not(outer))(lambda: run(False))

    for d in range(1, plane):
        sender = (ctx + d) % plane
        arrived(pos_slot(sender), pos_recv.at[sender])

    def partner(device):
        return device + 1 - 2 * core

    passed = []

    def lat_arrival(code, g):
        def got(target, recv):
            arrived(target, lat_recv.at[g, recv])

        def pass_on(target, recv, device):
            copy = lat_copy(g, recv, target, target, device)
            copy.start()
            passed.append(copy)

        if code == "xl":
            got(block(g, x_dev, 0, part), 0)
            pass_on(block(g, x_dev, 0, part), 5, y_dev)
        elif code == "yh":
            got(block(g, y_dev, part, part), 1)
            pass_on(block(g, y_dev, part, part), 6, x_dev)
        elif code == "xh":
            got(block(g, x_dev, part, part), 2)
            pass_on(block(g, x_dev), 7, mate)
        elif code == "yl":
            got(block(g, y_dev, 0, part), 3)
            pass_on(block(g, y_dev), 8, mate)
        elif code == "m":
            got(block(g, mate), 4)
        elif code == "dl":
            got(block(g, d_dev, 0, part), 5)
            pass_on(block(g, d_dev, 0, part), 9, mate)
        elif code == "dh":
            got(block(g, d_dev, part, part), 6)
            pass_on(block(g, d_dev, part, part), 10, mate)
        elif code == "mx":
            got(block(g, partner(x_dev)), 7)
        elif code == "my":
            got(block(g, partner(y_dev)), 8)
        elif code == "md":
            got(block(g, partner(d_dev), 0, part), 9)
            got(block(g, partner(d_dev), part, part), 10)

    scale = HD ** (-0.5) * math.log2(math.e)
    heads, strip = 2, 16
    chips = [ctx // 2, x_dev // 2, y_dev // 2, d_dev // 2]

    def project(c):
        base = pl.multiple_of(chips[c] * chip_rows, chip_rows)
        both = None
        for g in range(groups):
            term = jnp.dot(
                gathered[g, pl.ds(base, chip_rows), :], w_up[g * columns_each : (g + 1) * columns_each, :],
                preferred_element_type=jnp.float32,
            )
            both = term if both is None else both + term
        both = both.astype(jnp.bfloat16)
        dims = lax.broadcasted_iota(jnp.int32, (rows, chip_rows), 0)
        step = dims % half_rows
        own_block = jnp.where(dims // half_rows == 0, order_ref[0, 0], order_ref[0, 1])
        place = pos_all[0:1, pl.ds(base, chip_rows)]
        inside = jnp.logical_and(
            place // half_rows == own_block, jnp.logical_and(step == place % half_rows, step > 0)
        )
        later = jnp.logical_and(place // half_rows > own_block, step == 0)
        marks = jnp.where(jnp.logical_or(inside, later), 1.0, 0.0).T.astype(jnp.bfloat16)
        for g in range(KVH):
            keys[c, g, :, 0:HD] = both[:, g * HD : (g + 1) * HD]
            keys[c, g, :, HD : 2 * HD] = marks
            values[c, g, :, 0:HD] = both[:, (KVH + g) * HD : (KVH + g + 1) * HD]
            values[c, g, :, HD : 2 * HD] = jnp.ones((chip_rows, HD), jnp.bfloat16)

    sets = QH // heads
    size = heads * rows

    def where_of(i):
        return i * heads // share_heads, i * heads % share_heads * rows

    def score(c, i):
        g, first = where_of(i)
        return lax.dot_general(
            q_cat[g, first : first + size, :], keys[c, g], (((1,), (1,)), ((), ())),
            preferred_element_type=jnp.float32,
        )

    def weigh(c, i, scores):
        g, first = where_of(i)
        parts, scales = [], []
        for row in range(0, size, strip):
            kept = scores[row : row + strip]
            at = slice(first + row, first + row + strip)
            largest = jnp.broadcast_to(jnp.max(kept, axis=1, keepdims=True), (strip, HD))
            if c:
                before = highest[g, at, :]
                largest = jnp.maximum(largest, before)
                scales.append(jnp.exp2((before - largest) * scale))
            if c < len(chips) - 1:
                highest[g, at, :] = largest
            both = jnp.concatenate([largest] * (chip_rows // HD), axis=1)
            parts.append(jnp.exp2((kept - both) * scale).astype(jnp.bfloat16))
        summed = jnp.dot(jnp.concatenate(parts, axis=0), values[c, g], preferred_element_type=jnp.float32)
        if c:
            factor = jnp.concatenate(scales, axis=0)
            summed = summed + weighed[g, first : first + size, :] * jnp.concatenate([factor, factor], axis=1)
        if c < len(chips) - 1:
            weighed[g, first : first + size, :] = summed
        else:
            done = (summed[:, 0:HD] / summed[:, HD : 2 * HD]).astype(jnp.bfloat16)
            for k in range(heads):
                head = i * heads + k
                staged[:, head * HD : (head + 1) * HD] = done[k * rows : (k + 1) * rows]

    span = QH * HD // KVH

    def store(g):
        return pltpu.make_async_copy(
            staged.at[:, pl.ds(g * span, span)], out_ref.at[0, :, pl.ds(g * span, span)], out_sem.at[g]
        )

    each = sets // KVH
    for c, before in enumerate(TAIL):
        for event in before[0]:
            lat_arrival(*event)
        project(c)
        scores = score(c, 0)
        for i in range(sets):
            ahead = score(c, i + 1) if i + 1 < sets else None
            weigh(c, i, scores)
            scores = ahead
            for event in before[1].get(i, ()):
                lat_arrival(*event)
            if c == len(chips) - 1 and i % each == each - 1:
                store(i // each).start()

    for copy in passed:
        copy.wait_send()
    for g in range(groups):
        for index in range(4):
            departed(mine.at[g, pl.ds(0, part), :], lat_send.at[g, index])
        departed(mine.at[g], lat_send.at[g, 4])
    for d in range(1, plane):
        pos_copy(d).wait_send()

    def drain(end):
        for buffer, at, sems, index in drains[end]:
            departed(buffer.at[at], sems.at[index])

    pl.when(outer)(lambda: drain(True))
    pl.when(jnp.logical_not(outer))(lambda: drain(False))
    for g in range(KVH):
        store(g).wait()


def layer(tokens, w_down, w_up, queries, block_order):
    rows = tokens.shape[1]
    depth, width = w_down.shape
    each = width // 2
    chip_rows = 2 * rows
    dma = pltpu.SemaphoreType.DMA
    whole = pl.BlockSpec(memory_space=pltpu.HBM)
    bf16, f32 = jnp.bfloat16, jnp.float32
    return pl.pallas_call(
        layer_kernel,
        out_shape=jax.ShapeDtypeStruct(queries.shape, bf16),
        in_specs=[pl.BlockSpec(memory_space=pltpu.SMEM)] + [whole] * 4,
        out_specs=whole,
        scratch_shapes=[
            pltpu.VMEM((16, chip_rows, depth), bf16),
            pltpu.VMEM((4, chip_rows, depth), bf16),
            pltpu.VMEM((2, 16, depth, each), bf16),
            pltpu.VMEM((2, chip_rows, each), f32),
            pltpu.VMEM((2, chip_rows, each), f32),
            pltpu.VMEM((2, rows, each), f32),
            pltpu.VMEM((2, rows, each), f32),
            pltpu.VMEM((2, rows, each), f32),
            pltpu.VMEM((2, rows, each), f32),
            pltpu.VMEM((2, rows, each), bf16),
            pltpu.VMEM((2, 8 * rows, each), bf16),
            pltpu.VMEM((8, rows), jnp.int32),
            pltpu.VMEM((8, 8 * rows), jnp.int32),
            pltpu.VMEM(w_up.shape, bf16),
            pltpu.VMEM(queries.shape[1:], bf16),
            pltpu.VMEM((KVH, QH // KVH * rows, 2 * HD), bf16),
            pltpu.VMEM((4, KVH, chip_rows, 2 * HD), bf16),
            pltpu.VMEM((4, KVH, chip_rows, 2 * HD), bf16),
            pltpu.VMEM((KVH, QH // KVH * rows, 2 * HD), f32),
            pltpu.VMEM((KVH, QH // KVH * rows, HD), f32),
            pltpu.VMEM(queries.shape[1:], bf16),
            dma((16,)),
            dma((2,)),
            dma((16,)),
            dma((16,)),
            dma((8,)),
            dma((8,)),
            dma((160,)),
            dma((2, 16, 2)),
            dma((8,)),
            dma((8,)),
            dma((6,)),
            dma((6,)),
            dma((2, 11)),
            dma((2, 11)),
            dma((2,)),
            dma((KVH,)),
        ],
        compiler_params=pltpu.CompilerParams(
            collective_id=0, has_side_effects=True, vmem_limit_bytes=60 * 2**20
        ),
        name="layer",
    )(block_order, tokens, w_down, w_up, queries)


def per_device(layers, plane, tokens, w_down, w_up, queries, block_order):
    local_rows = tokens.shape[1]
    half_rows = local_rows // 2
    if plane == 8 and layers == 4:
        return layer(tokens, w_down, w_up, queries, block_order)
    summed = jnp.dot(
        tokens[0],
        lax.all_gather(w_down, ("dp", "ctx"), axis=0, tiled=True),
        preferred_element_type=jnp.float32,
    )
    latent = lax.all_gather(summed.astype(jnp.bfloat16), "ctx", axis=0, tiled=True)
    order = lax.all_gather(block_order, "ctx", axis=1, tiled=True)
    positions = jnp.repeat(order, half_rows, axis=1) * half_rows + jnp.tile(
        jnp.arange(half_rows, dtype=jnp.int32), order.shape[1]
    )
    return attend(block_order, positions, latent, w_up, queries)


def solution(mesh):
    placed = (
        P("dp", "ctx", None),
        P(("dp", "ctx"), None),
        P(),
        P("dp", "ctx", None),
        P("dp", "ctx"),
    )
    sizes = mesh.shape["dp"], mesh.shape["ctx"]
    return jax.shard_map(
        functools.partial(per_device, *sizes), mesh=mesh, in_specs=placed, out_specs=P("dp", "ctx", None), check_vma=False
    )
```

```python
import functools
import math

import jax
import jax.numpy as jnp
from jax import lax
from jax.experimental import pallas as pl
from jax.experimental.pallas import tpu as pltpu
from jax.sharding import PartitionSpec as P

QH = 32
KVH = 4
HD = 128
MESH = pl.DeviceIdType.MESH


def attention_kernel(order_ref, pos_ref, latent_ref, w_up_ref, q_ref, out_ref, keys, values, hidden):
    rows = q_ref.shape[1]
    count = latent_ref.shape[0]
    half = rows // 2
    tile = math.gcd(count, 256)

    @pl.loop(0, count // tile)
    def _(i):
        part = pl.ds(pl.multiple_of(i * tile, tile), tile)
        both = jnp.dot(
            latent_ref[part, :], w_up_ref[...], preferred_element_type=jnp.float32
        ).astype(jnp.bfloat16)
        for g in range(KVH):
            keys[g, part, 0:HD] = both[:, g * HD : (g + 1) * HD]
            values[g, part, 0:HD] = both[:, (KVH + g) * HD : (KVH + g + 1) * HD]
            values[g, part, HD : 2 * HD] = jnp.ones((tile, HD), jnp.bfloat16)
        dims = lax.broadcasted_iota(jnp.int32, (rows, tile), 0)
        first, step = dims // half, dims % half
        block = jnp.where(first == 0, order_ref[0, 0], order_ref[0, 1])
        place = pos_ref[0:1, part]
        inside = jnp.logical_and(place // half == block, jnp.logical_and(step == place % half, step > 0))
        later = jnp.logical_and(place // half > block, step == 0)
        marks = jnp.where(jnp.logical_or(inside, later), 1.0, 0.0).T.astype(jnp.bfloat16)
        for g in range(KVH):
            keys[g, part, HD : 2 * HD] = marks

    ids = lax.broadcasted_iota(jnp.int32, (rows, HD), 0)
    dims = lax.broadcasted_iota(jnp.int32, (rows, HD), 1)
    own = ids // half == dims // half
    blocked = jnp.logical_or(dims % half == 0, dims % half > ids % half)
    hidden[...] = jnp.where(jnp.logical_and(own, blocked), -1e30, 0.0).astype(jnp.bfloat16)
    scale = HD ** (-0.5) * math.log2(math.e)
    heads = 8
    group = QH // KVH

    def cols(first, width):
        return pl.ds(pl.multiple_of(first * HD, HD), width * HD)

    def score(i):
        queries = jnp.concatenate(
            [
                jnp.concatenate([q_ref[0, :, cols(i * heads + k, 1)], hidden[...]], axis=1)
                for k in range(heads)
            ],
            axis=0,
        )
        return lax.dot_general(
            queries,
            keys[i * heads // group],
            (((1,), (1,)), ((), ())),
            preferred_element_type=jnp.float32,
        )

    def weigh(i, scores):
        parts = []
        for first in range(0, heads * rows, strip):
            kept = scores[first : first + strip]
            largest = jnp.max(kept, axis=1, keepdims=True)
            parts.append(jnp.exp2((kept - largest) * scale).astype(jnp.bfloat16))
        summed = jnp.dot(
            jnp.concatenate(parts, axis=0),
            values[i * heads // group],
            preferred_element_type=jnp.float32,
        )
        summed = (summed[:, 0:HD] / summed[:, HD : 2 * HD]).astype(jnp.bfloat16)
        for k in range(heads):
            out_ref[0, :, cols(i * heads + k, 1)] = summed[k * rows : (k + 1) * rows]

    sets = QH // heads
    together = sets if count <= 1024 else 1
    strip = 16

    @pl.loop(0, sets // together)
    def _(i):
        scores = score(i * together)
        for k in range(together):
            ahead = score(i * together + k + 1) if k + 1 < together else None
            weigh(i * together + k, scores)
            scores = ahead


def attend(block_order, positions, latent, w_up, queries):
    count = latent.shape[0]
    rows = queries.shape[1]
    vmem = pl.BlockSpec(memory_space=pltpu.VMEM)
    return pl.pallas_call(
        attention_kernel,
        out_shape=jax.ShapeDtypeStruct(queries.shape, jnp.bfloat16),
        in_specs=[pl.BlockSpec(memory_space=pltpu.SMEM), vmem, vmem, vmem, vmem],
        out_specs=vmem,
        scratch_shapes=[
            pltpu.VMEM((KVH, count, 2 * HD), jnp.bfloat16),
            pltpu.VMEM((KVH, count, 2 * HD), jnp.bfloat16),
            pltpu.VMEM((rows, HD), jnp.bfloat16),
        ],
        compiler_params=pltpu.CompilerParams(vmem_limit_bytes=60 * 2**20),
        name="attention",
    )(block_order, positions, latent, w_up, queries)


PLACES = "sxyd"
HELPED = 2
MIRROR = {0: 3, 1: 2, 2: 1, 3: 0}
BY_Z = ((2, 0),)
IN_PLANE = ((3, 0), (3, 1), (1, 1))
END_STEPS = [
    ('tokens',), ('send', 0, 8), ('w', 0, 'x', 0, None), ('w', 0, 'y', 0, None), ('w', 1, 's', 0, None),
    ('w', 0, 'x', 1, None), ('w', 0, 'y', 1, None), ('w', 1, 's', 1, None), ('w', 0, 'd', 0, 0),
    ('w', 0, 'd', 0, 1), ('w', 1, 'x', 0, None), ('w', 1, 'y', 0, None), ('w', 0, 'd', 1, 0), ('w', 0, 'd', 1, 1),
    ('w', 3, 's', 0, None), ('w', 1, 'x', 1, None), ('w', 1, 'y', 1, None), ('w', 1, 'd', 0, 0),
    ('w', 1, 'd', 0, 1), ('w', 3, 'x', 0, None), ('w', 3, 'y', 0, None), ('w', 3, 's', 1, None),
    ('w', 1, 'd', 1, 0), ('w', 1, 'd', 1, 1), ('w', 3, 'd', 0, 0), ('w', 3, 'd', 0, 1), ('swap', 0),
    ('w', 3, 'x', 1, None), ('w', 3, 'y', 1, None), ('sum', 0), ('w', 3, 'd', 1, 0), ('w', 3, 'd', 1, 1),
    ('swap', 1), ('sum', 1),
]
INNER_STEPS = [
    ('tokens',), ('w', 0, 's', 0, None), ('w', 1, 'x', 0, None), ('w', 1, 'y', 0, None), ('w', 2, 's', 0, None),
    ('w', 0, 's', 1, None), ('w', 1, 'x', 1, None), ('w', 1, 'y', 1, None), ('w', 2, 's', 1, None),
    ('w', 0, 'x', 0, None), ('w', 0, 'y', 0, None), ('w', 3, 's', 0, None), ('w', 1, 'd', 0, 0),
    ('w', 2, 'x', 0, 1), ('w', 1, 'd', 0, 1), ('w', 2, 'y', 0, 1), ('w', 2, 'x', 0, 0), ('w', 2, 'y', 0, 0),
    ('w', 0, 'x', 1, None), ('w', 0, 'y', 1, None), ('w', 3, 's', 1, None), ('w', 1, 'd', 1, 0),
    ('w', 1, 'd', 1, 1), ('w', 2, 'd', 0, 0), ('w', 2, 'd', 0, 1), ('hswap', 0), ('w', 2, 'x', 1, None),
    ('w', 2, 'y', 1, None), ('w', 0, 'd', 0, 0), ('w', 2, 'd', 1, 0), ('part', 0), ('w', 0, 'd', 0, 1),
    ('w', 2, 'd', 1, 1), ('hswap', 1), ('w', 3, 'x', 0, None), ('w', 3, 'y', 0, None), ('w', 0, 'd', 1, 0),
    ('w', 3, 'd', 0, 0), ('part', 1), ('w', 0, 'd', 1, 1), ('w', 3, 'd', 0, 1), ('swap', 0), ('w', 3, 'x', 1, None),
    ('w', 3, 'y', 1, None), ('w', 3, 'd', 1, 0), ('sum', 0), ('w', 3, 'd', 1, 1), ('swap', 1), ('sum', 1),
]
TAIL = [
    ([("xl", 0), ("yh", 0), ("xh", 0), ("yl", 0), ("m", 0), ("m", 1)],
     {2: [("dl", 0), ("dh", 0)], 8: [("xl", 1), ("yh", 1)]}),
    ([("xh", 1), ("yl", 1)], {4: [("dl", 1), ("dh", 1)]}),
    ([("mx", 0), ("mx", 1), ("my", 0), ("my", 1)], {}),
    ([("md", 0), ("md", 1)], {}),
]


def route(end, piece):
    r, place, g, h = piece
    sends = []

    def to(link, r, place, h):
        sends.append((link, (r, place, g, h)))

    if place == "s":
        split = 0 if not end and (r, g) in BY_Z else None
        if end and r == 0:
            to("in", 0, "s", None)
        if not end and r == 1:
            to("in", 2, "s", None)
        if not end and r not in (0, HELPED):
            to("out", r, "s", None)
        to("x", r, "x", split)
        to("y", r, "y", split)
        if not end and r == 0:
            to("in", 3, "s", None)
    elif place in "xy":
        if r == (0 if end else 1) or (end and (r, g) in IN_PLANE):
            to(*(("y", r, "d", 0) if place == "x" else ("x", r, "d", 1)))
        if end and r == 0 and (0, g) in BY_Z:
            to("in", 0, place, 1)
        if not end and r == 0 and (3, g) in BY_Z and (h == 1 or (0, g) not in BY_Z):
            to("in", 3, place, 1)
        if not end and r == 1 and (2, g) in BY_Z:
            to("in", 2, place, 1)
    elif end:
        if r == 0:
            to("in", 0, "d", h)
    else:
        if r not in (0, HELPED) and (r, g) not in IN_PLANE:
            to("out", r, "d", h)
        if r in (0, 1):
            to("in", MIRROR[r], "d", h)
    return sends


def pieces(end, r, place, g):
    if place == "d" or (place in "xy" and not end and (r, g) in BY_Z):
        return 2
    return 1


def layer_kernel(
    order_ref, tokens_ref, w_ref, w_up_ref, q_ref, out_ref,
    tok, helped, w, acc, extra, share, extra_share, partial, ready, mine, gathered, pos_mine, pos_all,
    w_up, q_all, q_cat, keys, values, weighed, highest,
    load_sem, own_sem, tok_send, tok_recv, help_send, help_recv, w_send, w_recv,
    pos_send, pos_recv, sum_send, sum_recv, lat_send, lat_recv, late_sem,
):
    plane = 8
    z, ctx = lax.axis_index("dp"), lax.axis_index("ctx")
    core, x, y = ctx % 2, ctx // 2 % 2, ctx // 4
    mate = ctx + 1 - 2 * core
    x_dev, y_dev = ctx + 2 - 4 * x, ctx + 4 - 8 * y
    d_dev = (1 - y) * 4 + (1 - x) * 2 + core
    far = z // 2
    up = 1 - 2 * far
    rows, depth, width = tokens_ref.shape[1], w_ref.shape[0], w_ref.shape[1]
    groups = 2
    columns_each = width // groups
    half = depth // 2
    chip_rows = 2 * rows

    def feature(slot, side):
        r, bx, by = slot // 4, slot % 2, slot // 2 % 2
        chip = (y + by - 2 * y * by) * 2 + x + bx - 2 * x * bx
        layer = far * 3 + up * r
        return pl.ds(pl.multiple_of(((layer * 4 + chip) * 2 + side) * depth, depth), depth)

    def load(slot):
        return pltpu.make_async_copy(
            tokens_ref.at[0, :, feature(slot, core)], tok.at[slot, pl.ds(0, rows), :], load_sem.at[slot]
        )

    def swap(slot):
        return pltpu.make_async_remote_copy(
            tokens_ref.at[0, :, feature(slot, 1 - core)], tok.at[slot, pl.ds(rows, rows), :],
            tok_send.at[slot], tok_recv.at[slot], device_id=(z, mate), device_id_type=MESH,
        )

    def slot_of(r, place):
        return r * 4 + PLACES.index(place)

    def lines(h):
        return slice(None) if h is None else slice(h * half, h * half + half)

    def group_columns(g):
        return pl.ds(g * columns_each, columns_each)

    barrier = pltpu.get_barrier_semaphore()
    for d in range(1, plane):
        pl.semaphore_signal(barrier, inc=1, device_id=(z, (ctx + d) % plane), device_id_type=MESH)

    half_rows = rows // 2
    ids = lax.broadcasted_iota(jnp.int32, (8, rows), 1)
    pos_mine[...] = jnp.where(ids < half_rows, order_ref[0, 0], order_ref[0, 1]) * half_rows + ids % half_rows

    def pos_slot(device):
        return pos_all.at[:, pl.ds(pl.multiple_of(device * rows, rows), rows)]

    def pos_copy(d):
        return pltpu.make_async_remote_copy(
            pos_mine, pos_slot(ctx), pos_send.at[d], pos_recv.at[ctx],
            device_id=(z, (ctx + d) % plane), device_id_type=MESH,
        )

    def arrived(target, sem):
        pltpu.make_async_remote_copy(
            target, target, w_send.at[0], sem, device_id=(z, mate), device_id_type=MESH
        ).wait_recv()

    def departed(source, sem):
        pltpu.make_async_remote_copy(
            source, source, sem, pos_recv.at[0], device_id=(z, mate), device_id_type=MESH
        ).wait_send()

    part = rows // 2

    def block(g, device, first=0, size=rows):
        return gathered.at[g, pl.ds(pl.multiple_of(device * rows + first, part), size), :]

    def lat_copy(g, index, source, target, device):
        return pltpu.make_async_remote_copy(
            source, target, lat_send.at[g, index], lat_recv.at[g, index],
            device_id=(z, device), device_id_type=MESH,
        )

    late_loads = [
        pltpu.make_async_copy(w_up_ref, w_up, late_sem.at[0]),
        pltpu.make_async_copy(q_ref.at[0], q_all, late_sem.at[1]),
    ]

    def prepare_queries():
        late_loads[1].wait()
        ids = lax.broadcasted_iota(jnp.int32, (rows, HD), 0)
        dims = lax.broadcasted_iota(jnp.int32, (rows, HD), 1)
        own = ids // half_rows == dims // half_rows
        blocked = jnp.logical_or(dims % half_rows == 0, dims % half_rows > ids % half_rows)
        hidden = jnp.where(jnp.logical_and(own, blocked), -1e30, 0.0).astype(jnp.bfloat16)
        for head in range(QH):
            own_rows = pl.ds(head % share_heads * rows, rows)
            q_cat[head // share_heads, own_rows, 0:HD] = q_all[:, head * HD : (head + 1) * HD]
            q_cat[head // share_heads, own_rows, HD : 2 * HD] = hidden
        late_loads[0].wait()

    share_heads = QH // KVH

    def program(end):
        own_r = 0 if end else 1
        own = slot_of(own_r, "s")
        devices = {"x": (z, x_dev), "y": (z, y_dev), "in": (z + up, ctx), "out": (z - up, ctx)}
        if end:
            greeted = [(z + up, ctx), (z + up, mate)]
        else:
            greeted = [(z - up, ctx), (z - up, mate), (z + up, ctx)]
        for device in greeted:
            pl.semaphore_signal(barrier, inc=1, device_id=device, device_id_type=MESH)
        own_loads = [
            pltpu.make_async_copy(w_ref.at[:, group_columns(g)], w.at[g, own], own_sem.at[g]) for g in range(groups)
        ]
        for copy in own_loads:
            copy.start()
        pl.semaphore_wait(barrier, plane - 1 + len(greeted))

        sent = []

        def start(copy, *like):
            copy.start()
            sent.append(like)

        def forward(piece):
            for link, (r, place, g, h) in route(end, piece):
                at = (g, slot_of(r, place), lines(h), slice(None))
                target = w.at[at]
                if piece[:2] == (own_r, "s"):
                    source = w_ref.at[lines(h), group_columns(g)]
                else:
                    source = w.at[g, slot_of(*piece[:2]), lines(h), :]
                start(pltpu.make_async_remote_copy(
                    source, target, w_send.at[len(sent)], w_recv.at[g, slot_of(r, place), 1 if h == 1 else 0],
                    device_id=devices[link], device_id_type=MESH,
                ), w, at, w_send, len(sent))

        for g in range(groups):
            forward((own_r, "s", g, None))

        count = 12 if end else 16

        def used(i):
            return i + (i // (HELPED * 4)) * 4 if end else i

        def start_tokens(i, unused):
            swap(used(i)).start()
            load(used(i)).start()
            return unused

        lax.fori_loop(0, count, start_tokens, 0)

        for copy in late_loads:
            copy.start()
        for d in range(1, plane):
            pos_copy(d).start()
        pos_all[:, pl.ds(pl.multiple_of(ctx * rows, rows), rows)] = pos_mine[...]

        prepare_queries()

        def help_copy(i):
            place, other = i % 4, i // 4
            side = core + other - 2 * core * other
            return pltpu.make_async_remote_copy(
                tokens_ref.at[0, :, feature(HELPED * 4 + place, side)],
                helped.at[place, pl.ds(other * rows, rows), :],
                help_send.at[i], help_recv.at[i],
                device_id=(z + up, ctx if other == 0 else mate), device_id_type=MESH,
            )

        got, waiting, state = {}, [], {"tokens": False, "helped": False}

        def multiply(slot, g):
            acc[g] += jnp.dot(tok[slot], w[g, slot], preferred_element_type=jnp.float32)

        def w_arrival(r, place, g, h):
            slot = slot_of(r, place)
            arrived(w.at[g, slot, lines(h), :], w_recv.at[g, slot, 1 if h == 1 else 0])
            forward((r, place, g, h))
            got[slot, g] = got.get((slot, g), 0) + 1
            if got[slot, g] == pieces(end, r, place, g):
                if state["tokens"]:
                    multiply(slot, g)
                else:
                    waiting.append((slot, g))

        def tokens_arrival():
            def wait_tokens(i, unused):
                load(used(i)).wait()
                swap(used(i)).wait()
                return unused

            lax.fori_loop(0, count, wait_tokens, 0)
            for g in range(groups):
                own_loads[g].wait()
                acc[g] = jnp.dot(tok[own], w[g, own], preferred_element_type=jnp.float32)
            state["tokens"] = True
            for slot, g in waiting:
                multiply(slot, g)

        def help_send_some(first, last):
            for i in range(first, last):
                start(help_copy(i), helped, (i % 4, slice(i // 4 * rows, i // 4 * rows + rows)), help_send, i)

        def exchange(source, target, index):
            return pltpu.make_async_remote_copy(
                source, target, sum_send.at[index], sum_recv.at[index], device_id=(z, mate), device_id_type=MESH
            )

        def swap_sum(g):
            return exchange(acc.at[g, pl.ds(rows, rows), :], share.at[g], g)

        def swap_extra(g):
            return exchange(extra.at[g, pl.ds(rows, rows), :], extra_share.at[g], groups + g)

        def send_partial(g):
            return pltpu.make_async_remote_copy(
                ready.at[g], partial.at[g], sum_send.at[2 * groups + g], sum_recv.at[2 * groups + g],
                device_id=(z - up, ctx), device_id_type=MESH,
            )

        def start_swap(g):
            start(swap_sum(g), share, g, sum_send, g)

        def start_extra(g):
            if not state["helped"]:
                state["helped"] = True
                for i in range(8):
                    target = helped.at[i % 4, pl.ds(i // 4 * rows, rows), :]
                    arrived(target, help_recv.at[i])
            total = None
            for place in range(4):
                term = jnp.dot(helped[place], w[g, HELPED * 4 + place], preferred_element_type=jnp.float32)
                total = term if total is None else total + term
            extra[g] = total
            start(swap_extra(g), extra_share, g, sum_send, groups + g)

        def finish_extra(g):
            swap_extra(g).wait_recv()
            ready[g] = extra[g, 0:rows, :] + extra_share[g]
            start(send_partial(g), partial, g, sum_send, 2 * groups + g)

        def finish_sum(g):
            swap_sum(g).wait_recv()
            total = acc[g, 0:rows, :] + share[g]
            if end:
                send_partial(g).wait_recv()
                total = total + partial[g]
            mine[g] = total.astype(jnp.bfloat16)
            low, high = pl.ds(0, part), pl.ds(part, part)
            lat_copy(g, 0, mine.at[g, low, :], block(g, ctx, 0, part), x_dev).start()
            lat_copy(g, 1, mine.at[g, high, :], block(g, ctx, part, part), y_dev).start()
            lat_copy(g, 2, mine.at[g, high, :], block(g, ctx, part, part), x_dev).start()
            lat_copy(g, 3, mine.at[g, low, :], block(g, ctx, 0, part), y_dev).start()
            lat_copy(g, 4, mine.at[g], block(g, ctx), mate).start()
            gathered[g, pl.ds(pl.multiple_of(ctx * rows, rows), rows), :] = mine[g]

        steps = dict(
            w=w_arrival, tokens=tokens_arrival, send=help_send_some, swap=start_swap, sum=finish_sum,
            hswap=start_extra, part=finish_extra,
        )
        for kind, *where in END_STEPS if end else INNER_STEPS:
            steps[kind](*where)
        return sent

    outer = jnp.logical_or(z == 0, z == 3)
    drains = {}

    def run(end):
        drains[end] = program(end)

    pl.when(outer)(lambda: run(True))
    pl.when(jnp.logical_not(outer))(lambda: run(False))

    for d in range(1, plane):
        sender = (ctx + d) % plane
        arrived(pos_slot(sender), pos_recv.at[sender])

    def partner(device):
        return device + 1 - 2 * core

    passed = []

    def lat_arrival(code, g):
        def got(target, recv):
            arrived(target, lat_recv.at[g, recv])

        def pass_on(target, recv, device):
            copy = lat_copy(g, recv, target, target, device)
            copy.start()
            passed.append(copy)

        if code == "xl":
            got(block(g, x_dev, 0, part), 0)
            pass_on(block(g, x_dev, 0, part), 5, y_dev)
        elif code == "yh":
            got(block(g, y_dev, part, part), 1)
            pass_on(block(g, y_dev, part, part), 6, x_dev)
        elif code == "xh":
            got(block(g, x_dev, part, part), 2)
            pass_on(block(g, x_dev), 7, mate)
        elif code == "yl":
            got(block(g, y_dev, 0, part), 3)
            pass_on(block(g, y_dev), 8, mate)
        elif code == "m":
            got(block(g, mate), 4)
        elif code == "dl":
            got(block(g, d_dev, 0, part), 5)
            pass_on(block(g, d_dev, 0, part), 9, mate)
        elif code == "dh":
            got(block(g, d_dev, part, part), 6)
            pass_on(block(g, d_dev, part, part), 10, mate)
        elif code == "mx":
            got(block(g, partner(x_dev)), 7)
        elif code == "my":
            got(block(g, partner(y_dev)), 8)
        elif code == "md":
            got(block(g, partner(d_dev), 0, part), 9)
            got(block(g, partner(d_dev), part, part), 10)

    scale = HD ** (-0.5) * math.log2(math.e)
    heads, strip = 2, 16
    chunks = [(ctx, mate), (x_dev, y_dev), (partner(x_dev), partner(y_dev)), (d_dev, partner(d_dev))]

    def project(c):
        spans = [pl.ds(pl.multiple_of(device * rows, rows), rows) for device in chunks[c]]
        both = None
        for g in range(groups):
            term = jnp.dot(
                jnp.concatenate([gathered[g, span, :] for span in spans], axis=0),
                w_up[g * columns_each : (g + 1) * columns_each, :],
                preferred_element_type=jnp.float32,
            )
            both = term if both is None else both + term
        both = both.astype(jnp.bfloat16)
        dims = lax.broadcasted_iota(jnp.int32, (rows, chip_rows), 0)
        step = dims % half_rows
        own_block = jnp.where(dims // half_rows == 0, order_ref[0, 0], order_ref[0, 1])
        place = jnp.concatenate([pos_all[0:1, span] for span in spans], axis=1)
        inside = jnp.logical_and(
            place // half_rows == own_block, jnp.logical_and(step == place % half_rows, step > 0)
        )
        later = jnp.logical_and(place // half_rows > own_block, step == 0)
        marks = jnp.where(jnp.logical_or(inside, later), 1.0, 0.0).T.astype(jnp.bfloat16)
        for g in range(KVH):
            keys[c, g, :, 0:HD] = both[:, g * HD : (g + 1) * HD]
            keys[c, g, :, HD : 2 * HD] = marks
            values[c, g, :, 0:HD] = both[:, (KVH + g) * HD : (KVH + g + 1) * HD]
            values[c, g, :, HD : 2 * HD] = jnp.ones((chip_rows, HD), jnp.bfloat16)

    sets = QH // heads
    size = heads * rows

    def where_of(i):
        return i * heads // share_heads, i * heads % share_heads * rows

    def score(c, i):
        g, first = where_of(i)
        return lax.dot_general(
            q_cat[g, first : first + size, :], keys[c, g], (((1,), (1,)), ((), ())),
            preferred_element_type=jnp.float32,
        )

    def weigh(c, i, scores):
        g, first = where_of(i)
        parts, scales = [], []
        for row in range(0, size, strip):
            kept = scores[row : row + strip]
            at = slice(first + row, first + row + strip)
            largest = jnp.broadcast_to(jnp.max(kept, axis=1, keepdims=True), (strip, HD))
            if c:
                before = highest[g, at, :]
                largest = jnp.maximum(largest, before)
                scales.append(jnp.exp2((before - largest) * scale))
            if c < len(chunks) - 1:
                highest[g, at, :] = largest
            both = jnp.concatenate([largest] * (chip_rows // HD), axis=1)
            parts.append(jnp.exp2((kept - both) * scale).astype(jnp.bfloat16))
        summed = jnp.dot(jnp.concatenate(parts, axis=0), values[c, g], preferred_element_type=jnp.float32)
        if c:
            factor = jnp.concatenate(scales, axis=0)
            summed = summed + weighed[g, first : first + size, :] * jnp.concatenate([factor, factor], axis=1)
        if c < len(chunks) - 1:
            weighed[g, first : first + size, :] = summed
        else:
            done = (summed[:, 0:HD] / summed[:, HD : 2 * HD]).astype(jnp.bfloat16)
            for k in range(heads):
                head = i * heads + k
                out_ref[0, :, head * HD : (head + 1) * HD] = done[k * rows : (k + 1) * rows]

    for c, before in enumerate(TAIL):
        for event in before[0]:
            lat_arrival(*event)
        project(c)
        scores = score(c, 0)
        for i in range(sets):
            ahead = score(c, i + 1) if i + 1 < sets else None
            weigh(c, i, scores)
            scores = ahead
            for event in before[1].get(i, ()):
                lat_arrival(*event)

    for copy in passed:
        copy.wait_send()
    for g in range(groups):
        for index in range(4):
            departed(mine.at[g, pl.ds(0, part), :], lat_send.at[g, index])
        departed(mine.at[g], lat_send.at[g, 4])
    for d in range(1, plane):
        pos_copy(d).wait_send()

    def drain(end):
        for buffer, at, sems, index in drains[end]:
            departed(buffer.at[at], sems.at[index])

    pl.when(outer)(lambda: drain(True))
    pl.when(jnp.logical_not(outer))(lambda: drain(False))


def layer(tokens, w_down, w_up, queries, block_order):
    rows = tokens.shape[1]
    depth, width = w_down.shape
    each = width // 2
    chip_rows = 2 * rows
    dma = pltpu.SemaphoreType.DMA
    whole = pl.BlockSpec(memory_space=pltpu.HBM)
    bf16, f32 = jnp.bfloat16, jnp.float32
    return pl.pallas_call(
        layer_kernel,
        out_shape=pltpu.VMEM(queries.shape, bf16),
        in_specs=[pl.BlockSpec(memory_space=pltpu.SMEM)] + [whole] * 4,
        out_specs=pl.BlockSpec(memory_space=pltpu.VMEM),
        scratch_shapes=[
            pltpu.VMEM((16, chip_rows, depth), bf16),
            pltpu.VMEM((4, chip_rows, depth), bf16),
            pltpu.VMEM((2, 16, depth, each), bf16),
            pltpu.VMEM((2, chip_rows, each), f32),
            pltpu.VMEM((2, chip_rows, each), f32),
            pltpu.VMEM((2, rows, each), f32),
            pltpu.VMEM((2, rows, each), f32),
            pltpu.VMEM((2, rows, each), f32),
            pltpu.VMEM((2, rows, each), f32),
            pltpu.VMEM((2, rows, each), bf16),
            pltpu.VMEM((2, 8 * rows, each), bf16),
            pltpu.VMEM((8, rows), jnp.int32),
            pltpu.VMEM((8, 8 * rows), jnp.int32),
            pltpu.VMEM(w_up.shape, bf16),
            pltpu.VMEM(queries.shape[1:], bf16),
            pltpu.VMEM((KVH, QH // KVH * rows, 2 * HD), bf16),
            pltpu.VMEM((4, KVH, chip_rows, 2 * HD), bf16),
            pltpu.VMEM((4, KVH, chip_rows, 2 * HD), bf16),
            pltpu.VMEM((KVH, QH // KVH * rows, 2 * HD), f32),
            pltpu.VMEM((KVH, QH // KVH * rows, HD), f32),
            dma((16,)),
            dma((2,)),
            dma((16,)),
            dma((16,)),
            dma((8,)),
            dma((8,)),
            dma((160,)),
            dma((2, 16, 2)),
            dma((8,)),
            dma((8,)),
            dma((6,)),
            dma((6,)),
            dma((2, 11)),
            dma((2, 11)),
            dma((2,)),
        ],
        compiler_params=pltpu.CompilerParams(
            collective_id=0, has_side_effects=True, vmem_limit_bytes=50 * 2**20
        ),
        name="layer",
    )(*(pltpu.with_memory_space_constraint(a, pltpu.HBM) for a in (block_order, tokens, w_down, w_up, queries)))


def per_device(layers, plane, tokens, w_down, w_up, queries, block_order):
    local_rows = tokens.shape[1]
    half_rows = local_rows // 2
    if plane == 8 and layers == 4:
        return layer(tokens, w_down, w_up, queries, block_order)
    summed = jnp.dot(
        tokens[0],
        lax.all_gather(w_down, ("dp", "ctx"), axis=0, tiled=True),
        preferred_element_type=jnp.float32,
    )
    latent = lax.all_gather(summed.astype(jnp.bfloat16), "ctx", axis=0, tiled=True)
    order = lax.all_gather(block_order, "ctx", axis=1, tiled=True)
    positions = jnp.repeat(order, half_rows, axis=1) * half_rows + jnp.tile(
        jnp.arange(half_rows, dtype=jnp.int32), order.shape[1]
    )
    return attend(block_order, positions, latent, w_up, queries)


def solution(mesh):
    placed = (
        P("dp", "ctx", None),
        P(("dp", "ctx"), None),
        P(),
        P("dp", "ctx", None),
        P("dp", "ctx"),
    )
    sizes = mesh.shape["dp"], mesh.shape["ctx"]
    return jax.shard_map(
        functools.partial(per_device, *sizes), mesh=mesh, in_specs=placed, out_specs=P("dp", "ctx", None), check_vma=False
    )
```

```python
import functools
import math

import jax
import jax.numpy as jnp
from jax import lax
from jax.experimental import pallas as pl
from jax.experimental.pallas import tpu as pltpu
from jax.sharding import PartitionSpec as P

QH = 32
KVH = 4
HD = 128
MESH = pl.DeviceIdType.MESH


def attention_kernel(order_ref, pos_ref, latent_ref, w_up_ref, q_ref, out_ref, keys, values, hidden):
    rows = q_ref.shape[1]
    count = latent_ref.shape[0]
    half = rows // 2
    tile = math.gcd(count, 256)

    @pl.loop(0, count // tile)
    def _(i):
        part = pl.ds(pl.multiple_of(i * tile, tile), tile)
        both = jnp.dot(
            latent_ref[part, :], w_up_ref[...], preferred_element_type=jnp.float32
        ).astype(jnp.bfloat16)
        for g in range(KVH):
            keys[g, part, 0:HD] = both[:, g * HD : (g + 1) * HD]
            values[g, part, 0:HD] = both[:, (KVH + g) * HD : (KVH + g + 1) * HD]
            values[g, part, HD : 2 * HD] = jnp.ones((tile, HD), jnp.bfloat16)
        dims = lax.broadcasted_iota(jnp.int32, (rows, tile), 0)
        first, step = dims // half, dims % half
        block = jnp.where(first == 0, order_ref[0, 0], order_ref[0, 1])
        place = pos_ref[0:1, part]
        inside = jnp.logical_and(place // half == block, jnp.logical_and(step == place % half, step > 0))
        later = jnp.logical_and(place // half > block, step == 0)
        marks = jnp.where(jnp.logical_or(inside, later), 1.0, 0.0).T.astype(jnp.bfloat16)
        for g in range(KVH):
            keys[g, part, HD : 2 * HD] = marks

    ids = lax.broadcasted_iota(jnp.int32, (rows, HD), 0)
    dims = lax.broadcasted_iota(jnp.int32, (rows, HD), 1)
    own = ids // half == dims // half
    blocked = jnp.logical_or(dims % half == 0, dims % half > ids % half)
    hidden[...] = jnp.where(jnp.logical_and(own, blocked), -1e30, 0.0).astype(jnp.bfloat16)
    scale = HD ** (-0.5) * math.log2(math.e)
    heads = 8
    group = QH // KVH

    def cols(first, width):
        return pl.ds(pl.multiple_of(first * HD, HD), width * HD)

    def score(i):
        queries = jnp.concatenate(
            [
                jnp.concatenate([q_ref[0, :, cols(i * heads + k, 1)], hidden[...]], axis=1)
                for k in range(heads)
            ],
            axis=0,
        )
        return lax.dot_general(
            queries,
            keys[i * heads // group],
            (((1,), (1,)), ((), ())),
            preferred_element_type=jnp.float32,
        )

    def weigh(i, scores):
        parts = []
        for first in range(0, heads * rows, strip):
            kept = scores[first : first + strip]
            largest = jnp.max(kept, axis=1, keepdims=True)
            parts.append(jnp.exp2((kept - largest) * scale).astype(jnp.bfloat16))
        summed = jnp.dot(
            jnp.concatenate(parts, axis=0),
            values[i * heads // group],
            preferred_element_type=jnp.float32,
        )
        summed = (summed[:, 0:HD] / summed[:, HD : 2 * HD]).astype(jnp.bfloat16)
        for k in range(heads):
            out_ref[0, :, cols(i * heads + k, 1)] = summed[k * rows : (k + 1) * rows]

    sets = QH // heads
    together = sets if count <= 1024 else 1
    strip = 16

    @pl.loop(0, sets // together)
    def _(i):
        scores = score(i * together)
        for k in range(together):
            ahead = score(i * together + k + 1) if k + 1 < together else None
            weigh(i * together + k, scores)
            scores = ahead


def attend(block_order, positions, latent, w_up, queries):
    count = latent.shape[0]
    rows = queries.shape[1]
    vmem = pl.BlockSpec(memory_space=pltpu.VMEM)
    return pl.pallas_call(
        attention_kernel,
        out_shape=jax.ShapeDtypeStruct(queries.shape, jnp.bfloat16),
        in_specs=[pl.BlockSpec(memory_space=pltpu.SMEM), vmem, vmem, vmem, vmem],
        out_specs=vmem,
        scratch_shapes=[
            pltpu.VMEM((KVH, count, 2 * HD), jnp.bfloat16),
            pltpu.VMEM((KVH, count, 2 * HD), jnp.bfloat16),
            pltpu.VMEM((rows, HD), jnp.bfloat16),
        ],
        compiler_params=pltpu.CompilerParams(vmem_limit_bytes=60 * 2**20),
        name="attention",
    )(block_order, positions, latent, w_up, queries)


PLACES = "sxyd"
HELPED = 2
MIRROR = {0: 3, 1: 2, 2: 1, 3: 0}
BY_Z = ((2, 0),)
IN_PLANE = ((3, 0), (3, 1), (1, 1))
END_STEPS = [
    ('tokens',), ('send', 0, 8), ('w', 0, 'x', 0, None), ('w', 0, 'y', 0, None), ('w', 1, 's', 0, None),
    ('w', 0, 'x', 1, None), ('w', 0, 'y', 1, None), ('w', 1, 's', 1, None), ('marks',), ('w', 0, 'd', 0, 0),
    ('w', 0, 'd', 0, 1), ('w', 1, 'x', 0, None), ('w', 1, 'y', 0, None), ('w', 0, 'd', 1, 0), ('w', 0, 'd', 1, 1),
    ('w', 3, 's', 0, None), ('w', 1, 'x', 1, None), ('w', 1, 'y', 1, None), ('w', 1, 'd', 0, 0),
    ('w', 1, 'd', 0, 1), ('w', 3, 'x', 0, None), ('w', 3, 'y', 0, None), ('w', 3, 's', 1, None),
    ('w', 1, 'd', 1, 0), ('w', 1, 'd', 1, 1), ('w', 3, 'd', 0, 0), ('w', 3, 'd', 0, 1), ('got', 0), ('swap', 0),
    ('w', 3, 'x', 1, None), ('w', 3, 'y', 1, None), ('sum', 0), ('w', 3, 'd', 1, 0), ('w', 3, 'd', 1, 1),
    ('got', 1), ('swap', 1), ('sum', 1),
]
INNER_STEPS = [
    ('tokens',), ('w', 0, 's', 0, None), ('w', 1, 'x', 0, None), ('w', 1, 'y', 0, None), ('w', 2, 's', 0, None),
    ('w', 0, 's', 1, None), ('w', 1, 'x', 1, None), ('w', 1, 'y', 1, None), ('w', 2, 's', 1, None),
    ('w', 0, 'x', 0, None), ('w', 0, 'y', 0, None), ('w', 3, 's', 0, None), ('marks',), ('w', 1, 'd', 0, 0),
    ('w', 2, 'x', 0, 1), ('w', 1, 'd', 0, 1), ('w', 2, 'y', 0, 1), ('w', 2, 'x', 0, 0), ('w', 2, 'y', 0, 0),
    ('w', 0, 'x', 1, None), ('w', 0, 'y', 1, None), ('w', 3, 's', 1, None), ('w', 1, 'd', 1, 0),
    ('w', 1, 'd', 1, 1), ('w', 2, 'd', 0, 0), ('w', 2, 'd', 0, 1), ('hswap', 0), ('w', 2, 'x', 1, None),
    ('w', 2, 'y', 1, None), ('w', 0, 'd', 0, 0), ('w', 2, 'd', 1, 0), ('part', 0), ('w', 0, 'd', 0, 1),
    ('w', 2, 'd', 1, 1), ('hswap', 1), ('w', 3, 'x', 0, None), ('w', 3, 'y', 0, None), ('w', 0, 'd', 1, 0),
    ('w', 3, 'd', 0, 0), ('part', 1), ('w', 0, 'd', 1, 1), ('w', 3, 'd', 0, 1), ('swap', 0), ('w', 3, 'x', 1, None),
    ('w', 3, 'y', 1, None), ('w', 3, 'd', 1, 0), ('sum', 0), ('w', 3, 'd', 1, 1), ('swap', 1), ('sum', 1),
]
TAIL = [
    ([("xl", 0), ("yh", 0), ("xh", 0), ("yl", 0)],
     {2: [("dl", 0), ("dh", 0)], 8: [("xl", 1), ("yh", 1)]}),
    ([("xh", 1), ("yl", 1)], {4: [("dl", 1), ("dh", 1)]}),
    ([("mx", 0), ("mx", 1), ("my", 0), ("my", 1)], {}),
    ([("md", 0), ("md", 1)], {}),
]


def route(end, piece):
    r, place, g, h = piece
    sends = []

    def to(link, r, place, h):
        sends.append((link, (r, place, g, h)))

    if place == "s":
        split = 0 if not end and (r, g) in BY_Z else None
        if end and r == 0:
            to("in", 0, "s", None)
        if not end and r == 1:
            to("in", 2, "s", None)
        if not end and r not in (0, HELPED):
            to("out", r, "s", None)
        to("x", r, "x", split)
        to("y", r, "y", split)
        if not end and r == 0:
            to("in", 3, "s", None)
    elif place in "xy":
        if r == (0 if end else 1) or (end and (r, g) in IN_PLANE):
            to(*(("y", r, "d", 0) if place == "x" else ("x", r, "d", 1)))
        if end and r == 0 and (0, g) in BY_Z:
            to("in", 0, place, 1)
        if not end and r == 0 and (3, g) in BY_Z and (h == 1 or (0, g) not in BY_Z):
            to("in", 3, place, 1)
        if not end and r == 1 and (2, g) in BY_Z:
            to("in", 2, place, 1)
    elif end:
        if r == 0:
            to("in", 0, "d", h)
    else:
        if r not in (0, HELPED) and (r, g) not in IN_PLANE:
            to("out", r, "d", h)
        if r in (0, 1):
            to("in", MIRROR[r], "d", h)
    return sends


def pieces(end, r, place, g):
    if place == "d" or (place in "xy" and not end and (r, g) in BY_Z):
        return 2
    return 1


def layer_kernel(
    order_ref, tokens_ref, w_ref, w_up_ref, q_ref, out_ref,
    tok, helped, w, acc, swapped, extra, share, extra_share, partial, ready, mine, gathered, pos_mine, pos_all,
    w_up, q_all, q_cat, keys, values, weighed, highest,
    load_sem, own_sem, tok_send, tok_recv, help_send, help_recv, w_send, w_recv,
    pos_send, pos_recv, sum_send, sum_recv, lat_send, lat_recv, late_sem,
):
    plane = 8
    z, ctx = lax.axis_index("dp"), lax.axis_index("ctx")
    core, x, y = ctx % 2, ctx // 2 % 2, ctx // 4
    mate = ctx + 1 - 2 * core
    x_dev, y_dev = ctx + 2 - 4 * x, ctx + 4 - 8 * y
    d_dev = (1 - y) * 4 + (1 - x) * 2 + core
    far = z // 2
    up = 1 - 2 * far
    rows, depth, width = tokens_ref.shape[1], w_ref.shape[0], w_ref.shape[1]
    groups = 2
    columns_each = width // groups
    half = depth // 2
    chip_rows = 2 * rows

    def feature(slot, side):
        r, bx, by = slot // 4, slot % 2, slot // 2 % 2
        chip = (y + by - 2 * y * by) * 2 + x + bx - 2 * x * bx
        layer = far * 3 + up * r
        return pl.ds(pl.multiple_of(((layer * 4 + chip) * 2 + side) * depth, depth), depth)

    def load(slot):
        return pltpu.make_async_copy(
            tokens_ref.at[0, :, feature(slot, core)], tok.at[slot, pl.ds(0, rows), :], load_sem.at[slot]
        )

    def swap(slot):
        return pltpu.make_async_remote_copy(
            tokens_ref.at[0, :, feature(slot, 1 - core)], tok.at[slot, pl.ds(rows, rows), :],
            tok_send.at[slot], tok_recv.at[slot], device_id=(z, mate), device_id_type=MESH,
        )

    def slot_of(r, place):
        return r * 4 + PLACES.index(place)

    def lines(h):
        return slice(None) if h is None else slice(h * half, h * half + half)

    def group_columns(g):
        return pl.ds(g * columns_each, columns_each)

    barrier = pltpu.get_barrier_semaphore()
    for d in range(1, plane):
        pl.semaphore_signal(barrier, inc=1, device_id=(z, (ctx + d) % plane), device_id_type=MESH)

    half_rows = rows // 2
    ids = lax.broadcasted_iota(jnp.int32, (8, rows), 1)
    pos_mine[...] = jnp.where(ids < half_rows, order_ref[0, 0], order_ref[0, 1]) * half_rows + ids % half_rows

    def pos_slot(device):
        return pos_all.at[:, pl.ds(pl.multiple_of(device * rows, rows), rows)]

    def pos_copy(d):
        return pltpu.make_async_remote_copy(
            pos_mine, pos_slot(ctx), pos_send.at[d], pos_recv.at[ctx],
            device_id=(z, (ctx + d) % plane), device_id_type=MESH,
        )

    def arrived(target, sem):
        pltpu.make_async_remote_copy(
            target, target, w_send.at[0], sem, device_id=(z, mate), device_id_type=MESH
        ).wait_recv()

    def departed(source, sem):
        pltpu.make_async_remote_copy(
            source, source, sem, pos_recv.at[0], device_id=(z, mate), device_id_type=MESH
        ).wait_send()

    part = rows // 2

    def block(g, device, first=0, size=rows):
        return gathered.at[g, pl.ds(pl.multiple_of(device * rows + first, part), size), :]

    def lat_copy(g, index, source, target, device):
        return pltpu.make_async_remote_copy(
            source, target, lat_send.at[g, index], lat_recv.at[g, index],
            device_id=(z, device), device_id_type=MESH,
        )

    late_loads = [
        pltpu.make_async_copy(w_up_ref, w_up, late_sem.at[0]),
        pltpu.make_async_copy(q_ref.at[0], q_all, late_sem.at[1]),
    ]

    def prepare_queries():
        late_loads[1].wait()
        ids = lax.broadcasted_iota(jnp.int32, (rows, HD), 0)
        dims = lax.broadcasted_iota(jnp.int32, (rows, HD), 1)
        own = ids // half_rows == dims // half_rows
        blocked = jnp.logical_or(dims % half_rows == 0, dims % half_rows > ids % half_rows)
        hidden = jnp.where(jnp.logical_and(own, blocked), -1e30, 0.0).astype(jnp.bfloat16)
        for head in range(QH):
            own_rows = pl.ds(head % share_heads * rows, rows)
            q_cat[head // share_heads, own_rows, 0:HD] = q_all[:, head * HD : (head + 1) * HD]
            q_cat[head // share_heads, own_rows, HD : 2 * HD] = hidden
        late_loads[0].wait()

    share_heads = QH // KVH

    def partner(device):
        return device + 1 - 2 * core

    chunks = [(ctx, mate), (x_dev, y_dev), (partner(x_dev), partner(y_dev)), (d_dev, partner(d_dev))]

    def spans_of(c):
        return [pl.ds(pl.multiple_of(device * rows, rows), rows) for device in chunks[c]]

    def prepare_marks():
        for d in range(1, plane):
            sender = (ctx + d) % plane
            arrived(pos_slot(sender), pos_recv.at[sender])
        for c in range(len(chunks)):
            dims = lax.broadcasted_iota(jnp.int32, (rows, chip_rows), 0)
            step = dims % half_rows
            own_block = jnp.where(dims // half_rows == 0, order_ref[0, 0], order_ref[0, 1])
            place = jnp.concatenate([pos_all[0:1, span] for span in spans_of(c)], axis=1)
            inside = jnp.logical_and(
                place // half_rows == own_block, jnp.logical_and(step == place % half_rows, step > 0)
            )
            later = jnp.logical_and(place // half_rows > own_block, step == 0)
            marks = jnp.where(jnp.logical_or(inside, later), 1.0, 0.0).T.astype(jnp.bfloat16)
            for g in range(KVH):
                keys[c, g, :, HD : 2 * HD] = marks
                values[c, g, :, HD : 2 * HD] = jnp.ones((chip_rows, HD), jnp.bfloat16)

    def program(end):
        own_r = 0 if end else 1
        own = slot_of(own_r, "s")
        devices = {"x": (z, x_dev), "y": (z, y_dev), "in": (z + up, ctx), "out": (z - up, ctx)}
        if end:
            greeted = [(z + up, ctx), (z + up, mate)]
        else:
            greeted = [(z - up, ctx), (z - up, mate), (z + up, ctx)]
        for device in greeted:
            pl.semaphore_signal(barrier, inc=1, device_id=device, device_id_type=MESH)
        own_loads = [
            pltpu.make_async_copy(w_ref.at[:, group_columns(g)], w.at[g, own], own_sem.at[g]) for g in range(groups)
        ]
        for copy in own_loads:
            copy.start()
        pl.semaphore_wait(barrier, plane - 1 + len(greeted))

        sent = []

        def start(copy, *like):
            copy.start()
            sent.append(like)

        def forward(piece):
            for link, (r, place, g, h) in route(end, piece):
                at = (g, slot_of(r, place), lines(h), slice(None))
                target = w.at[at]
                if piece[:2] == (own_r, "s"):
                    source = w_ref.at[lines(h), group_columns(g)]
                else:
                    source = w.at[g, slot_of(*piece[:2]), lines(h), :]
                start(pltpu.make_async_remote_copy(
                    source, target, w_send.at[len(sent)], w_recv.at[g, slot_of(r, place), 1 if h == 1 else 0],
                    device_id=devices[link], device_id_type=MESH,
                ), w, at, w_send, len(sent))

        for g in range(groups):
            forward((own_r, "s", g, None))

        count = 12 if end else 16

        def used(i):
            return i + (i // (HELPED * 4)) * 4 if end else i

        def start_tokens(i, unused):
            swap(used(i)).start()
            load(used(i)).start()
            return unused

        lax.fori_loop(0, count, start_tokens, 0)

        for copy in late_loads:
            copy.start()
        for d in range(1, plane):
            pos_copy(d).start()
        pos_all[:, pl.ds(pl.multiple_of(ctx * rows, rows), rows)] = pos_mine[...]

        prepare_queries()

        def help_copy(i):
            place, other = i % 4, i // 4
            side = core + other - 2 * core * other
            return pltpu.make_async_remote_copy(
                tokens_ref.at[0, :, feature(HELPED * 4 + place, side)],
                helped.at[place, pl.ds(other * rows, rows), :],
                help_send.at[i], help_recv.at[i],
                device_id=(z + up, ctx if other == 0 else mate), device_id_type=MESH,
            )

        got, waiting, state = {}, [], {"tokens": False, "helped": False}

        def multiply(slot, g):
            acc[g] += jnp.dot(tok[slot], w[g, slot], preferred_element_type=jnp.float32)

        def w_arrival(r, place, g, h):
            slot = slot_of(r, place)
            arrived(w.at[g, slot, lines(h), :], w_recv.at[g, slot, 1 if h == 1 else 0])
            forward((r, place, g, h))
            got[slot, g] = got.get((slot, g), 0) + 1
            if got[slot, g] == pieces(end, r, place, g):
                if state["tokens"]:
                    multiply(slot, g)
                else:
                    waiting.append((slot, g))

        def tokens_arrival():
            def wait_tokens(i, unused):
                load(used(i)).wait()
                swap(used(i)).wait()
                return unused

            lax.fori_loop(0, count, wait_tokens, 0)
            for g in range(groups):
                own_loads[g].wait()
                acc[g] = jnp.dot(tok[own], w[g, own], preferred_element_type=jnp.float32)
            state["tokens"] = True
            for slot, g in waiting:
                multiply(slot, g)

        def help_send_some(first, last):
            for i in range(first, last):
                start(help_copy(i), helped, (i % 4, slice(i // 4 * rows, i // 4 * rows + rows)), help_send, i)

        def exchange(source, target, index):
            return pltpu.make_async_remote_copy(
                source, target, sum_send.at[index], sum_recv.at[index], device_id=(z, mate), device_id_type=MESH
            )

        def swap_sum(g):
            return exchange(swapped.at[g], share.at[g], g)

        def swap_extra(g):
            return exchange(extra.at[g, pl.ds(rows, rows), :], extra_share.at[g], groups + g)

        def send_partial(g):
            return pltpu.make_async_remote_copy(
                ready.at[g], partial.at[g, pl.ds(0, rows), :], sum_send.at[2 * groups + g], sum_recv.at[2 * groups + g],
                device_id=(z - up, ctx), device_id_type=MESH,
            )

        def pass_partial(g):
            return exchange(partial.at[g, pl.ds(0, rows), :], partial.at[g, pl.ds(rows, rows), :], 3 * groups + g)

        def partial_arrival(g):
            send_partial(g).wait_recv()
            start(pass_partial(g), ready, g, sum_send, 3 * groups + g)

        def start_swap(g):
            swapped[g, 0:rows, :] = acc[g, rows:chip_rows, :]
            swapped[g, rows:chip_rows, :] = acc[g, 0:rows, :]
            start(swap_sum(g), share, g, sum_send, g)

        def start_extra(g):
            if not state["helped"]:
                state["helped"] = True
                for i in range(8):
                    target = helped.at[i % 4, pl.ds(i // 4 * rows, rows), :]
                    arrived(target, help_recv.at[i])
            total = None
            for place in range(4):
                term = jnp.dot(helped[place], w[g, HELPED * 4 + place], preferred_element_type=jnp.float32)
                total = term if total is None else total + term
            extra[g] = total
            start(swap_extra(g), extra_share, g, sum_send, groups + g)

        def finish_extra(g):
            swap_extra(g).wait_recv()
            ready[g] = extra[g, 0:rows, :] + extra_share[g]
            start(send_partial(g), ready, g, sum_send, 2 * groups + g)

        def finish_sum(g):
            swap_sum(g).wait_recv()
            total = acc[g] + share[g]
            if end:
                pass_partial(g).wait_recv()
                total = total + partial[g]
            total = total.astype(jnp.bfloat16)
            mine[g] = total[0:rows]
            low, high = pl.ds(0, part), pl.ds(part, part)
            lat_copy(g, 0, mine.at[g, low, :], block(g, ctx, 0, part), x_dev).start()
            lat_copy(g, 1, mine.at[g, high, :], block(g, ctx, part, part), y_dev).start()
            lat_copy(g, 2, mine.at[g, high, :], block(g, ctx, part, part), x_dev).start()
            lat_copy(g, 3, mine.at[g, low, :], block(g, ctx, 0, part), y_dev).start()
            gathered[g, pl.ds(pl.multiple_of(ctx * rows, rows), rows), :] = total[0:rows]
            gathered[g, pl.ds(pl.multiple_of(mate * rows, rows), rows), :] = total[rows:chip_rows]

        steps = dict(
            w=w_arrival, tokens=tokens_arrival, marks=prepare_marks, send=help_send_some, swap=start_swap, sum=finish_sum,
            hswap=start_extra, part=finish_extra, got=partial_arrival,
        )
        for kind, *where in END_STEPS if end else INNER_STEPS:
            steps[kind](*where)
        return sent

    outer = jnp.logical_or(z == 0, z == 3)
    drains = {}

    def run(end):
        drains[end] = program(end)

    pl.when(outer)(lambda: run(True))
    pl.when(jnp.logical_not(outer))(lambda: run(False))

    passed = []

    def lat_arrival(code, g):
        def got(target, recv):
            arrived(target, lat_recv.at[g, recv])

        def pass_on(target, recv, device):
            copy = lat_copy(g, recv, target, target, device)
            copy.start()
            passed.append(copy)

        if code == "xl":
            got(block(g, x_dev, 0, part), 0)
            pass_on(block(g, x_dev, 0, part), 5, y_dev)
        elif code == "yh":
            got(block(g, y_dev, part, part), 1)
            pass_on(block(g, y_dev, part, part), 6, x_dev)
        elif code == "xh":
            got(block(g, x_dev, part, part), 2)
            pass_on(block(g, x_dev), 7, mate)
        elif code == "yl":
            got(block(g, y_dev, 0, part), 3)
            pass_on(block(g, y_dev), 8, mate)
        elif code == "dl":
            got(block(g, d_dev, 0, part), 5)
            pass_on(block(g, d_dev, 0, part), 9, mate)
        elif code == "dh":
            got(block(g, d_dev, part, part), 6)
            pass_on(block(g, d_dev, part, part), 10, mate)
        elif code == "mx":
            got(block(g, partner(x_dev)), 7)
        elif code == "my":
            got(block(g, partner(y_dev)), 8)
        elif code == "md":
            got(block(g, partner(d_dev), 0, part), 9)
            got(block(g, partner(d_dev), part, part), 10)

    scale = HD ** (-0.5) * math.log2(math.e)
    heads, strip = 2, 16

    def project(c):
        spans = spans_of(c)
        both = None
        for g in range(groups):
            term = jnp.dot(
                jnp.concatenate([gathered[g, span, :] for span in spans], axis=0),
                w_up[g * columns_each : (g + 1) * columns_each, :],
                preferred_element_type=jnp.float32,
            )
            both = term if both is None else both + term
        both = both.astype(jnp.bfloat16)
        for g in range(KVH):
            keys[c, g, :, 0:HD] = both[:, g * HD : (g + 1) * HD]
            values[c, g, :, 0:HD] = both[:, (KVH + g) * HD : (KVH + g + 1) * HD]

    sets = QH // heads
    size = heads * rows

    def where_of(i):
        return i * heads // share_heads, i * heads % share_heads * rows

    def score(c, i):
        g, first = where_of(i)
        return lax.dot_general(
            q_cat[g, first : first + size, :], keys[c, g], (((1,), (1,)), ((), ())),
            preferred_element_type=jnp.float32,
        )

    def weigh(c, i, scores):
        g, first = where_of(i)
        parts, scales = [], []
        for row in range(0, size, strip):
            kept = scores[row : row + strip]
            at = slice(first + row, first + row + strip)
            largest = jnp.broadcast_to(jnp.max(kept, axis=1, keepdims=True), (strip, HD))
            if c:
                before = highest[g, at, :]
                largest = jnp.maximum(largest, before)
                scales.append(jnp.exp2((before - largest) * scale))
            if c < len(chunks) - 1:
                highest[g, at, :] = largest
            both = jnp.concatenate([largest] * (chip_rows // HD), axis=1)
            parts.append(jnp.exp2((kept - both) * scale).astype(jnp.bfloat16))
        summed = jnp.dot(jnp.concatenate(parts, axis=0), values[c, g], preferred_element_type=jnp.float32)
        if c:
            factor = jnp.concatenate(scales, axis=0)
            summed = summed + weighed[g, first : first + size, :] * jnp.concatenate([factor, factor], axis=1)
        if c < len(chunks) - 1:
            weighed[g, first : first + size, :] = summed
        else:
            done = (summed[:, 0:HD] / summed[:, HD : 2 * HD]).astype(jnp.bfloat16)
            for k in range(heads):
                head = i * heads + k
                out_ref[0, :, head * HD : (head + 1) * HD] = done[k * rows : (k + 1) * rows]

    for c, before in enumerate(TAIL):
        for event in before[0]:
            lat_arrival(*event)
        project(c)
        scores = score(c, 0)
        for i in range(sets):
            ahead = score(c, i + 1) if i + 1 < sets else None
            weigh(c, i, scores)
            scores = ahead
            for event in before[1].get(i, ()):
                lat_arrival(*event)

    for copy in passed:
        copy.wait_send()
    for g in range(groups):
        for index in range(4):
            departed(mine.at[g, pl.ds(0, part), :], lat_send.at[g, index])
    for d in range(1, plane):
        pos_copy(d).wait_send()

    def drain(end):
        for buffer, at, sems, index in drains[end]:
            departed(buffer.at[at], sems.at[index])

    pl.when(outer)(lambda: drain(True))
    pl.when(jnp.logical_not(outer))(lambda: drain(False))


def layer(tokens, w_down, w_up, queries, block_order):
    rows = tokens.shape[1]
    depth, width = w_down.shape
    each = width // 2
    chip_rows = 2 * rows
    dma = pltpu.SemaphoreType.DMA
    whole = pl.BlockSpec(memory_space=pltpu.HBM)
    bf16, f32 = jnp.bfloat16, jnp.float32
    return pl.pallas_call(
        layer_kernel,
        out_shape=pltpu.VMEM(queries.shape, bf16),
        in_specs=[pl.BlockSpec(memory_space=pltpu.SMEM)] + [whole] * 4,
        out_specs=pl.BlockSpec(memory_space=pltpu.VMEM),
        scratch_shapes=[
            pltpu.VMEM((16, chip_rows, depth), bf16),
            pltpu.VMEM((4, chip_rows, depth), bf16),
            pltpu.VMEM((2, 16, depth, each), bf16),
            pltpu.VMEM((2, chip_rows, each), f32),
            pltpu.VMEM((2, chip_rows, each), f32),
            pltpu.VMEM((2, chip_rows, each), f32),
            pltpu.VMEM((2, chip_rows, each), f32),
            pltpu.VMEM((2, rows, each), f32),
            pltpu.VMEM((2, chip_rows, each), f32),
            pltpu.VMEM((2, rows, each), f32),
            pltpu.VMEM((2, rows, each), bf16),
            pltpu.VMEM((2, 8 * rows, each), bf16),
            pltpu.VMEM((8, rows), jnp.int32),
            pltpu.VMEM((8, 8 * rows), jnp.int32),
            pltpu.VMEM(w_up.shape, bf16),
            pltpu.VMEM(queries.shape[1:], bf16),
            pltpu.VMEM((KVH, QH // KVH * rows, 2 * HD), bf16),
            pltpu.VMEM((4, KVH, chip_rows, 2 * HD), bf16),
            pltpu.VMEM((4, KVH, chip_rows, 2 * HD), bf16),
            pltpu.VMEM((KVH, QH // KVH * rows, 2 * HD), f32),
            pltpu.VMEM((KVH, QH // KVH * rows, HD), f32),
            dma((16,)),
            dma((2,)),
            dma((16,)),
            dma((16,)),
            dma((8,)),
            dma((8,)),
            dma((160,)),
            dma((2, 16, 2)),
            dma((8,)),
            dma((8,)),
            dma((8,)),
            dma((8,)),
            dma((2, 11)),
            dma((2, 11)),
            dma((2,)),
        ],
        compiler_params=pltpu.CompilerParams(
            collective_id=0, has_side_effects=True, vmem_limit_bytes=50 * 2**20
        ),
        name="layer",
    )(*(pltpu.with_memory_space_constraint(a, pltpu.HBM) for a in (block_order, tokens, w_down, w_up, queries)))


def per_device(layers, plane, tokens, w_down, w_up, queries, block_order):
    local_rows = tokens.shape[1]
    half_rows = local_rows // 2
    if plane == 8 and layers == 4:
        return layer(tokens, w_down, w_up, queries, block_order)
    summed = jnp.dot(
        tokens[0],
        lax.all_gather(w_down, ("dp", "ctx"), axis=0, tiled=True),
        preferred_element_type=jnp.float32,
    )
    latent = lax.all_gather(summed.astype(jnp.bfloat16), "ctx", axis=0, tiled=True)
    order = lax.all_gather(block_order, "ctx", axis=1, tiled=True)
    positions = jnp.repeat(order, half_rows, axis=1) * half_rows + jnp.tile(
        jnp.arange(half_rows, dtype=jnp.int32), order.shape[1]
    )
    return attend(block_order, positions, latent, w_up, queries)


def solution(mesh):
    placed = (
        P("dp", "ctx", None),
        P(("dp", "ctx"), None),
        P(),
        P("dp", "ctx", None),
        P("dp", "ctx"),
    )
    sizes = mesh.shape["dp"], mesh.shape["ctx"]
    return jax.shard_map(
        functools.partial(per_device, *sizes), mesh=mesh, in_specs=placed, out_specs=P("dp", "ctx", None), check_vma=False
    )
```

```python
import functools
import math

import jax
import jax.numpy as jnp
from jax import lax
from jax.experimental import pallas as pl
from jax.experimental.pallas import tpu as pltpu
from jax.sharding import PartitionSpec as P

QH = 32
KVH = 4
HD = 128
MESH = pl.DeviceIdType.MESH


def attention_kernel(order_ref, pos_ref, latent_ref, w_up_ref, q_ref, out_ref, keys, values, hidden):
    rows = q_ref.shape[1]
    count = latent_ref.shape[0]
    half = rows // 2
    tile = math.gcd(count, 256)

    @pl.loop(0, count // tile)
    def _(i):
        part = pl.ds(pl.multiple_of(i * tile, tile), tile)
        both = jnp.dot(
            latent_ref[part, :], w_up_ref[...], preferred_element_type=jnp.float32
        ).astype(jnp.bfloat16)
        for g in range(KVH):
            keys[g, part, 0:HD] = both[:, g * HD : (g + 1) * HD]
            values[g, part, 0:HD] = both[:, (KVH + g) * HD : (KVH + g + 1) * HD]
            values[g, part, HD : 2 * HD] = jnp.ones((tile, HD), jnp.bfloat16)
        dims = lax.broadcasted_iota(jnp.int32, (rows, tile), 0)
        first, step = dims // half, dims % half
        block = jnp.where(first == 0, order_ref[0, 0], order_ref[0, 1])
        place = pos_ref[0:1, part]
        inside = jnp.logical_and(place // half == block, jnp.logical_and(step == place % half, step > 0))
        later = jnp.logical_and(place // half > block, step == 0)
        marks = jnp.where(jnp.logical_or(inside, later), 1.0, 0.0).T.astype(jnp.bfloat16)
        for g in range(KVH):
            keys[g, part, HD : 2 * HD] = marks

    ids = lax.broadcasted_iota(jnp.int32, (rows, HD), 0)
    dims = lax.broadcasted_iota(jnp.int32, (rows, HD), 1)
    own = ids // half == dims // half
    blocked = jnp.logical_or(dims % half == 0, dims % half > ids % half)
    hidden[...] = jnp.where(jnp.logical_and(own, blocked), -1e30, 0.0).astype(jnp.bfloat16)
    scale = HD ** (-0.5) * math.log2(math.e)
    heads = 8
    group = QH // KVH

    def cols(first, width):
        return pl.ds(pl.multiple_of(first * HD, HD), width * HD)

    def score(i):
        queries = jnp.concatenate(
            [
                jnp.concatenate([q_ref[0, :, cols(i * heads + k, 1)], hidden[...]], axis=1)
                for k in range(heads)
            ],
            axis=0,
        )
        return lax.dot_general(
            queries,
            keys[i * heads // group],
            (((1,), (1,)), ((), ())),
            preferred_element_type=jnp.float32,
        )

    def weigh(i, scores):
        parts = []
        for first in range(0, heads * rows, strip):
            kept = scores[first : first + strip]
            largest = jnp.max(kept, axis=1, keepdims=True)
            parts.append(jnp.exp2((kept - largest) * scale).astype(jnp.bfloat16))
        summed = jnp.dot(
            jnp.concatenate(parts, axis=0),
            values[i * heads // group],
            preferred_element_type=jnp.float32,
        )
        summed = (summed[:, 0:HD] / summed[:, HD : 2 * HD]).astype(jnp.bfloat16)
        for k in range(heads):
            out_ref[0, :, cols(i * heads + k, 1)] = summed[k * rows : (k + 1) * rows]

    sets = QH // heads
    together = sets if count <= 1024 else 1
    strip = 16

    @pl.loop(0, sets // together)
    def _(i):
        scores = score(i * together)
        for k in range(together):
            ahead = score(i * together + k + 1) if k + 1 < together else None
            weigh(i * together + k, scores)
            scores = ahead


def attend(block_order, positions, latent, w_up, queries):
    count = latent.shape[0]
    rows = queries.shape[1]
    vmem = pl.BlockSpec(memory_space=pltpu.VMEM)
    return pl.pallas_call(
        attention_kernel,
        out_shape=jax.ShapeDtypeStruct(queries.shape, jnp.bfloat16),
        in_specs=[pl.BlockSpec(memory_space=pltpu.SMEM), vmem, vmem, vmem, vmem],
        out_specs=vmem,
        scratch_shapes=[
            pltpu.VMEM((KVH, count, 2 * HD), jnp.bfloat16),
            pltpu.VMEM((KVH, count, 2 * HD), jnp.bfloat16),
            pltpu.VMEM((rows, HD), jnp.bfloat16),
        ],
        compiler_params=pltpu.CompilerParams(vmem_limit_bytes=60 * 2**20),
        name="attention",
    )(block_order, positions, latent, w_up, queries)


PLACES = "sxyd"
HELPED = 2
MIRROR = {0: 3, 1: 2, 2: 1, 3: 0}
BY_Z = ((2, 0),)
IN_PLANE = ((3, 0), (3, 1), (1, 1))
END_STEPS = [
    ('tokens',), ('send', 0, 8), ('w', 0, 'x', 0, None), ('w', 0, 'y', 0, None), ('w', 1, 's', 0, None),
    ('w', 0, 'x', 1, None), ('w', 0, 'y', 1, None), ('w', 1, 's', 1, None), ('marks',), ('w', 0, 'd', 0, 0),
    ('w', 0, 'd', 0, 1), ('w', 1, 'x', 0, None), ('w', 1, 'y', 0, None), ('w', 0, 'd', 1, 0), ('w', 0, 'd', 1, 1),
    ('w', 3, 's', 0, None), ('w', 1, 'x', 1, None), ('w', 1, 'y', 1, None), ('w', 1, 'd', 0, 0),
    ('w', 1, 'd', 0, 1), ('w', 3, 'x', 0, None), ('w', 3, 'y', 0, None), ('w', 3, 's', 1, None),
    ('w', 1, 'd', 1, 0), ('w', 1, 'd', 1, 1), ('w', 3, 'd', 0, 0), ('w', 3, 'd', 0, 1), ('got', 0), ('swap', 0),
    ('w', 3, 'x', 1, None), ('w', 3, 'y', 1, None), ('sum', 0), ('w', 3, 'd', 1, 0), ('w', 3, 'd', 1, 1),
    ('got', 1), ('swap', 1), ('sum', 1),
]
INNER_STEPS = [
    ('tokens',), ('w', 0, 's', 0, None), ('w', 1, 'x', 0, None), ('w', 1, 'y', 0, None), ('w', 2, 's', 0, None),
    ('w', 0, 's', 1, None), ('w', 1, 'x', 1, None), ('w', 1, 'y', 1, None), ('w', 2, 's', 1, None),
    ('w', 0, 'x', 0, None), ('w', 0, 'y', 0, None), ('w', 3, 's', 0, None), ('marks',), ('w', 1, 'd', 0, 0),
    ('w', 2, 'x', 0, 1), ('w', 1, 'd', 0, 1), ('w', 2, 'y', 0, 1), ('w', 2, 'x', 0, 0), ('w', 2, 'y', 0, 0),
    ('w', 0, 'x', 1, None), ('w', 0, 'y', 1, None), ('w', 3, 's', 1, None), ('w', 1, 'd', 1, 0),
    ('w', 1, 'd', 1, 1), ('w', 2, 'd', 0, 0), ('w', 2, 'd', 0, 1), ('hswap', 0), ('w', 2, 'x', 1, None),
    ('w', 2, 'y', 1, None), ('w', 0, 'd', 0, 0), ('w', 2, 'd', 1, 0), ('part', 0), ('w', 0, 'd', 0, 1),
    ('w', 2, 'd', 1, 1), ('hswap', 1), ('w', 3, 'x', 0, None), ('w', 3, 'y', 0, None), ('w', 0, 'd', 1, 0),
    ('w', 3, 'd', 0, 0), ('part', 1), ('w', 0, 'd', 1, 1), ('w', 3, 'd', 0, 1), ('swap', 0), ('w', 3, 'x', 1, None),
    ('w', 3, 'y', 1, None), ('w', 3, 'd', 1, 0), ('sum', 0), ('w', 3, 'd', 1, 1), ('swap', 1), ('sum', 1),
]
TAIL = [
    ([("xl", 0), ("yh", 0), ("xh", 0), ("yl", 0)], {4: [("dl", 0), ("dh", 0)], 11: [("xl", 1), ("yh", 1)], 15: [("xh", 1), ("yl", 1)]}),
    ([], {9: [("dl", 1), ("dh", 1)]}),
    ([("mx", 0), ("mx", 1), ("my", 0), ("my", 1)], {}),
    ([("md", 0), ("md", 1)], {}),
]


def route(end, piece):
    r, place, g, h = piece
    sends = []

    def to(link, r, place, h):
        sends.append((link, (r, place, g, h)))

    if place == "s":
        split = 0 if not end and (r, g) in BY_Z else None
        if end and r == 0:
            to("in", 0, "s", None)
        if not end and r == 1:
            to("in", 2, "s", None)
        if not end and r not in (0, HELPED):
            to("out", r, "s", None)
        to("x", r, "x", split)
        to("y", r, "y", split)
        if not end and r == 0:
            to("in", 3, "s", None)
    elif place in "xy":
        if r == (0 if end else 1) or (end and (r, g) in IN_PLANE):
            to(*(("y", r, "d", 0) if place == "x" else ("x", r, "d", 1)))
        if end and r == 0 and (0, g) in BY_Z:
            to("in", 0, place, 1)
        if not end and r == 0 and (3, g) in BY_Z and (h == 1 or (0, g) not in BY_Z):
            to("in", 3, place, 1)
        if not end and r == 1 and (2, g) in BY_Z:
            to("in", 2, place, 1)
    elif end:
        if r == 0:
            to("in", 0, "d", h)
    else:
        if r not in (0, HELPED) and (r, g) not in IN_PLANE:
            to("out", r, "d", h)
        if r in (0, 1):
            to("in", MIRROR[r], "d", h)
    return sends


def pieces(end, r, place, g):
    if place == "d" or (place in "xy" and not end and (r, g) in BY_Z):
        return 2
    return 1


def layer_kernel(
    order_ref, tokens_ref, w_ref, w_up_ref, q_ref, out_ref,
    tok, helped, w, acc, extra, share, extra_share, partial, ready, mine, gathered, pos_mine, pos_all,
    w_up, q_all, q_cat, keys, values, weighed, highest,
    load_sem, own_sem, tok_send, tok_recv, help_send, help_recv, w_send, w_recv,
    pos_send, pos_recv, sum_send, sum_recv, lat_send, lat_recv, late_sem,
):
    plane = 8
    z, ctx = lax.axis_index("dp"), lax.axis_index("ctx")
    core, x, y = ctx % 2, ctx // 2 % 2, ctx // 4
    mate = ctx + 1 - 2 * core
    x_dev, y_dev = ctx + 2 - 4 * x, ctx + 4 - 8 * y
    d_dev = (1 - y) * 4 + (1 - x) * 2 + core
    far = z // 2
    up = 1 - 2 * far
    rows, depth, width = tokens_ref.shape[1], w_ref.shape[0], w_ref.shape[1]
    groups = 2
    columns_each = width // groups
    half = depth // 2
    chip_rows = 2 * rows

    def feature(slot, side):
        r, bx, by = slot // 4, slot % 2, slot // 2 % 2
        chip = (y + by - 2 * y * by) * 2 + x + bx - 2 * x * bx
        layer = far * 3 + up * r
        return pl.ds(pl.multiple_of(((layer * 4 + chip) * 2 + side) * depth, depth), depth)

    def load(slot):
        return pltpu.make_async_copy(
            tokens_ref.at[0, :, feature(slot, core)], tok.at[slot, pl.ds(0, rows), :], load_sem.at[slot]
        )

    def swap(slot):
        return pltpu.make_async_remote_copy(
            tokens_ref.at[0, :, feature(slot, 1 - core)], tok.at[slot, pl.ds(rows, rows), :],
            tok_send.at[slot], tok_recv.at[slot], device_id=(z, mate), device_id_type=MESH,
        )

    def slot_of(r, place):
        return r * 4 + PLACES.index(place)

    def lines(h):
        return slice(None) if h is None else slice(h * half, h * half + half)

    def group_columns(g):
        return pl.ds(g * columns_each, columns_each)

    barrier = pltpu.get_barrier_semaphore()
    for d in range(1, plane):
        pl.semaphore_signal(barrier, inc=1, device_id=(z, (ctx + d) % plane), device_id_type=MESH)

    half_rows = rows // 2
    ids = lax.broadcasted_iota(jnp.int32, (8, rows), 1)
    pos_mine[...] = jnp.where(ids < half_rows, order_ref[0, 0], order_ref[0, 1]) * half_rows + ids % half_rows

    def pos_slot(device):
        return pos_all.at[:, pl.ds(pl.multiple_of(device * rows, rows), rows)]

    def pos_copy(d):
        return pltpu.make_async_remote_copy(
            pos_mine, pos_slot(ctx), pos_send.at[d], pos_recv.at[ctx],
            device_id=(z, (ctx + d) % plane), device_id_type=MESH,
        )

    def arrived(target, sem):
        pltpu.make_async_remote_copy(
            target, target, w_send.at[0], sem, device_id=(z, mate), device_id_type=MESH
        ).wait_recv()

    def departed(source, sem):
        pltpu.make_async_remote_copy(
            source, source, sem, pos_recv.at[0], device_id=(z, mate), device_id_type=MESH
        ).wait_send()

    part = rows // 2

    def block(g, device, first=0, size=rows):
        return gathered.at[g, pl.ds(pl.multiple_of(device * rows + first, part), size), :]

    def lat_copy(g, index, source, target, device):
        return pltpu.make_async_remote_copy(
            source, target, lat_send.at[g, index], lat_recv.at[g, index],
            device_id=(z, device), device_id_type=MESH,
        )

    late_loads = [
        pltpu.make_async_copy(w_up_ref, w_up, late_sem.at[0]),
        pltpu.make_async_copy(q_ref.at[0], q_all, late_sem.at[1]),
    ]

    def prepare_queries():
        late_loads[1].wait()
        ids = lax.broadcasted_iota(jnp.int32, (rows, HD), 0)
        dims = lax.broadcasted_iota(jnp.int32, (rows, HD), 1)
        own = ids // half_rows == dims // half_rows
        blocked = jnp.logical_or(dims % half_rows == 0, dims % half_rows > ids % half_rows)
        hidden = jnp.where(jnp.logical_and(own, blocked), -1e30, 0.0).astype(jnp.bfloat16)
        for head in range(QH):
            own_rows = pl.ds(head % share_heads * rows, rows)
            q_cat[head // share_heads, own_rows, 0:HD] = q_all[:, head * HD : (head + 1) * HD]
            q_cat[head // share_heads, own_rows, HD : 2 * HD] = hidden
        late_loads[0].wait()

    share_heads = QH // KVH

    def partner(device):
        return device + 1 - 2 * core

    chunks = [(ctx, mate), (x_dev, y_dev), (partner(x_dev), partner(y_dev)), (d_dev, partner(d_dev))]

    def spans_of(c):
        return [pl.ds(pl.multiple_of(device * rows, rows), rows) for device in chunks[c]]

    def prepare_marks():
        for d in range(1, plane):
            sender = (ctx + d) % plane
            arrived(pos_slot(sender), pos_recv.at[sender])
        for c in range(len(chunks)):
            dims = lax.broadcasted_iota(jnp.int32, (rows, chip_rows), 0)
            step = dims % half_rows
            own_block = jnp.where(dims // half_rows == 0, order_ref[0, 0], order_ref[0, 1])
            place = jnp.concatenate([pos_all[0:1, span] for span in spans_of(c)], axis=1)
            inside = jnp.logical_and(
                place // half_rows == own_block, jnp.logical_and(step == place % half_rows, step > 0)
            )
            later = jnp.logical_and(place // half_rows > own_block, step == 0)
            marks = jnp.where(jnp.logical_or(inside, later), 1.0, 0.0).T.astype(jnp.bfloat16)
            for g in range(KVH):
                keys[c, g, :, HD : 2 * HD] = marks
                values[c, g, :, HD : 2 * HD] = jnp.ones((chip_rows, HD), jnp.bfloat16)

    def program(end):
        own_r = 0 if end else 1
        own = slot_of(own_r, "s")
        devices = {"x": (z, x_dev), "y": (z, y_dev), "in": (z + up, ctx), "out": (z - up, ctx)}
        if end:
            greeted = [(z + up, ctx), (z + up, mate)]
        else:
            greeted = [(z - up, ctx), (z - up, mate), (z + up, ctx)]
        for device in greeted:
            pl.semaphore_signal(barrier, inc=1, device_id=device, device_id_type=MESH)
        own_loads = [
            pltpu.make_async_copy(w_ref.at[:, group_columns(g)], w.at[g, own], own_sem.at[g]) for g in range(groups)
        ]
        for copy in own_loads:
            copy.start()
        pl.semaphore_wait(barrier, plane - 1 + len(greeted))

        sent = []

        def start(copy, *like):
            copy.start()
            sent.append(like)

        def forward(piece):
            for link, (r, place, g, h) in route(end, piece):
                at = (g, slot_of(r, place), lines(h), slice(None))
                target = w.at[at]
                if piece[:2] == (own_r, "s"):
                    source = w_ref.at[lines(h), group_columns(g)]
                else:
                    source = w.at[g, slot_of(*piece[:2]), lines(h), :]
                start(pltpu.make_async_remote_copy(
                    source, target, w_send.at[len(sent)], w_recv.at[g, slot_of(r, place), 1 if h == 1 else 0],
                    device_id=devices[link], device_id_type=MESH,
                ), w, at, w_send, len(sent))

        for g in range(groups):
            forward((own_r, "s", g, None))

        count = 12 if end else 16

        def used(i):
            return i + (i // (HELPED * 4)) * 4 if end else i

        def start_tokens(i, unused):
            swap(used(i)).start()
            load(used(i)).start()
            return unused

        lax.fori_loop(0, count, start_tokens, 0)

        for copy in late_loads:
            copy.start()
        for d in range(1, plane):
            pos_copy(d).start()
        pos_all[:, pl.ds(pl.multiple_of(ctx * rows, rows), rows)] = pos_mine[...]

        prepare_queries()

        def help_copy(i):
            place, other = i % 4, i // 4
            side = core + other - 2 * core * other
            return pltpu.make_async_remote_copy(
                tokens_ref.at[0, :, feature(HELPED * 4 + place, side)],
                helped.at[place, pl.ds(other * rows, rows), :],
                help_send.at[i], help_recv.at[i],
                device_id=(z + up, ctx if other == 0 else mate), device_id_type=MESH,
            )

        got, waiting, state = {}, [], {"tokens": False, "helped": False}

        def multiply(slot, g):
            acc[g] += jnp.dot(tok[slot], w[g, slot], preferred_element_type=jnp.float32)

        def w_arrival(r, place, g, h):
            slot = slot_of(r, place)
            arrived(w.at[g, slot, lines(h), :], w_recv.at[g, slot, 1 if h == 1 else 0])
            forward((r, place, g, h))
            got[slot, g] = got.get((slot, g), 0) + 1
            if got[slot, g] == pieces(end, r, place, g):
                if state["tokens"]:
                    multiply(slot, g)
                else:
                    waiting.append((slot, g))

        def tokens_arrival():
            def wait_tokens(i, unused):
                load(used(i)).wait()
                swap(used(i)).wait()
                return unused

            lax.fori_loop(0, count, wait_tokens, 0)
            for g in range(groups):
                own_loads[g].wait()
                acc[g] = jnp.dot(tok[own], w[g, own], preferred_element_type=jnp.float32)
            state["tokens"] = True
            for slot, g in waiting:
                multiply(slot, g)

        def help_send_some(first, last):
            for i in range(first, last):
                start(help_copy(i), helped, (i % 4, slice(i // 4 * rows, i // 4 * rows + rows)), help_send, i)

        def exchange(source, target, index):
            return pltpu.make_async_remote_copy(
                source, target, sum_send.at[index], sum_recv.at[index], device_id=(z, mate), device_id_type=MESH
            )

        def swap_sum(g, second):
            first, other = (rows, 0) if second == 0 else (0, rows)
            return exchange(
                acc.at[g, pl.ds(first, rows), :], share.at[g, pl.ds(other, rows), :],
                g if second == 0 else 4 * groups + g,
            )

        def swap_extra(g):
            return exchange(extra.at[g, pl.ds(rows, rows), :], extra_share.at[g], groups + g)

        def send_partial(g):
            return pltpu.make_async_remote_copy(
                ready.at[g], partial.at[g, pl.ds(0, rows), :], sum_send.at[2 * groups + g], sum_recv.at[2 * groups + g],
                device_id=(z - up, ctx), device_id_type=MESH,
            )

        def pass_partial(g):
            return exchange(partial.at[g, pl.ds(0, rows), :], partial.at[g, pl.ds(rows, rows), :], 3 * groups + g)

        def partial_arrival(g):
            send_partial(g).wait_recv()
            start(pass_partial(g), ready, g, sum_send, 3 * groups + g)

        def start_swap(g):
            start(swap_sum(g, 0), ready, g, sum_send, g)
            start(swap_sum(g, 1), ready, g, sum_send, 4 * groups + g)

        def start_extra(g):
            if not state["helped"]:
                state["helped"] = True
                for i in range(8):
                    target = helped.at[i % 4, pl.ds(i // 4 * rows, rows), :]
                    arrived(target, help_recv.at[i])
            total = None
            for place in range(4):
                term = jnp.dot(helped[place], w[g, HELPED * 4 + place], preferred_element_type=jnp.float32)
                total = term if total is None else total + term
            extra[g] = total
            start(swap_extra(g), extra_share, g, sum_send, groups + g)

        def finish_extra(g):
            swap_extra(g).wait_recv()
            ready[g] = extra[g, 0:rows, :] + extra_share[g]
            start(send_partial(g), ready, g, sum_send, 2 * groups + g)

        def finish_sum(g):
            swap_sum(g, 0).wait_recv()
            total = acc[g, 0:rows, :] + share[g, 0:rows, :]
            if end:
                total = total + partial[g, 0:rows, :]
            mine[g] = total.astype(jnp.bfloat16)
            low, high = pl.ds(0, part), pl.ds(part, part)
            lat_copy(g, 0, mine.at[g, low, :], block(g, ctx, 0, part), x_dev).start()
            lat_copy(g, 1, mine.at[g, high, :], block(g, ctx, part, part), y_dev).start()
            lat_copy(g, 2, mine.at[g, high, :], block(g, ctx, part, part), x_dev).start()
            lat_copy(g, 3, mine.at[g, low, :], block(g, ctx, 0, part), y_dev).start()
            gathered[g, pl.ds(pl.multiple_of(ctx * rows, rows), rows), :] = mine[g]
            swap_sum(g, 1).wait_recv()
            total = acc[g, rows:chip_rows, :] + share[g, rows:chip_rows, :]
            if end:
                pass_partial(g).wait_recv()
                total = total + partial[g, rows:chip_rows, :]
            gathered[g, pl.ds(pl.multiple_of(mate * rows, rows), rows), :] = total.astype(jnp.bfloat16)

        steps = dict(
            w=w_arrival, tokens=tokens_arrival, marks=prepare_marks, send=help_send_some, swap=start_swap, sum=finish_sum,
            hswap=start_extra, part=finish_extra, got=partial_arrival,
        )
        for kind, *where in END_STEPS if end else INNER_STEPS:
            steps[kind](*where)
        return sent

    outer = jnp.logical_or(z == 0, z == 3)
    drains = {}

    def run(end):
        drains[end] = program(end)

    pl.when(outer)(lambda: run(True))
    pl.when(jnp.logical_not(outer))(lambda: run(False))

    passed = []

    def lat_arrival(code, g):
        def got(target, recv):
            arrived(target, lat_recv.at[g, recv])

        def pass_on(target, recv, device):
            copy = lat_copy(g, recv, target, target, device)
            copy.start()
            passed.append(copy)

        if code == "xl":
            got(block(g, x_dev, 0, part), 0)
            pass_on(block(g, x_dev, 0, part), 5, y_dev)
        elif code == "yh":
            got(block(g, y_dev, part, part), 1)
            pass_on(block(g, y_dev, part, part), 6, x_dev)
        elif code == "xh":
            got(block(g, x_dev, part, part), 2)
            pass_on(block(g, x_dev), 7, mate)
        elif code == "yl":
            got(block(g, y_dev, 0, part), 3)
            pass_on(block(g, y_dev), 8, mate)
        elif code == "dl":
            got(block(g, d_dev, 0, part), 5)
            pass_on(block(g, d_dev, 0, part), 9, mate)
        elif code == "dh":
            got(block(g, d_dev, part, part), 6)
            pass_on(block(g, d_dev, part, part), 10, mate)
        elif code == "mx":
            got(block(g, partner(x_dev)), 7)
        elif code == "my":
            got(block(g, partner(y_dev)), 8)
        elif code == "md":
            got(block(g, partner(d_dev), 0, part), 9)
            got(block(g, partner(d_dev), part, part), 10)

    scale = HD ** (-0.5) * math.log2(math.e)
    heads, strip = 2, 16

    def project(c):
        spans = spans_of(c)
        both = None
        for g in range(groups):
            term = jnp.dot(
                jnp.concatenate([gathered[g, span, :] for span in spans], axis=0),
                w_up[g * columns_each : (g + 1) * columns_each, :],
                preferred_element_type=jnp.float32,
            )
            both = term if both is None else both + term
        both = both.astype(jnp.bfloat16)
        for g in range(KVH):
            keys[c, g, :, 0:HD] = both[:, g * HD : (g + 1) * HD]
            values[c, g, :, 0:HD] = both[:, (KVH + g) * HD : (KVH + g + 1) * HD]

    sets = QH // heads
    size = heads * rows

    def where_of(i):
        return i * heads // share_heads, i * heads % share_heads * rows

    def score(c, i):
        g, first = where_of(i)
        return lax.dot_general(
            q_cat[g, first : first + size, :], keys[c, g], (((1,), (1,)), ((), ())),
            preferred_element_type=jnp.float32,
        )

    def weigh(c, i, scores):
        g, first = where_of(i)
        parts, scales = [], []
        for row in range(0, size, strip):
            kept = scores[row : row + strip]
            at = slice(first + row, first + row + strip)
            largest = jnp.broadcast_to(jnp.max(kept, axis=1, keepdims=True), (strip, HD))
            if c:
                before = highest[g, at, :]
                largest = jnp.maximum(largest, before)
                scales.append(jnp.exp2((before - largest) * scale))
            if c < len(chunks) - 1:
                highest[g, at, :] = largest
            both = jnp.concatenate([largest] * (chip_rows // HD), axis=1)
            parts.append(jnp.exp2((kept - both) * scale).astype(jnp.bfloat16))
        summed = jnp.dot(jnp.concatenate(parts, axis=0), values[c, g], preferred_element_type=jnp.float32)
        if c:
            factor = jnp.concatenate(scales, axis=0)
            summed = summed + weighed[g, first : first + size, :] * jnp.concatenate([factor, factor], axis=1)
        if c < len(chunks) - 1:
            weighed[g, first : first + size, :] = summed
        else:
            done = (summed[:, 0:HD] / summed[:, HD : 2 * HD]).astype(jnp.bfloat16)
            for k in range(heads):
                head = i * heads + k
                out_ref[0, :, head * HD : (head + 1) * HD] = done[k * rows : (k + 1) * rows]

    for c, before in enumerate(TAIL):
        for event in before[0]:
            lat_arrival(*event)
        project(c)
        scores = score(c, 0)
        for i in range(sets):
            ahead = score(c, i + 1) if i + 1 < sets else None
            weigh(c, i, scores)
            scores = ahead
            for event in before[1].get(i, ()):
                lat_arrival(*event)

    for copy in passed:
        copy.wait_send()
    for g in range(groups):
        for index in range(4):
            departed(mine.at[g, pl.ds(0, part), :], lat_send.at[g, index])
    for d in range(1, plane):
        pos_copy(d).wait_send()

    def drain(end):
        for buffer, at, sems, index in drains[end]:
            departed(buffer.at[at], sems.at[index])

    pl.when(outer)(lambda: drain(True))
    pl.when(jnp.logical_not(outer))(lambda: drain(False))


def layer(tokens, w_down, w_up, queries, block_order):
    rows = tokens.shape[1]
    depth, width = w_down.shape
    each = width // 2
    chip_rows = 2 * rows
    dma = pltpu.SemaphoreType.DMA
    whole = pl.BlockSpec(memory_space=pltpu.HBM)
    bf16, f32 = jnp.bfloat16, jnp.float32
    return pl.pallas_call(
        layer_kernel,
        out_shape=pltpu.VMEM(queries.shape, bf16),
        in_specs=[pl.BlockSpec(memory_space=pltpu.SMEM)] + [whole] * 4,
        out_specs=pl.BlockSpec(memory_space=pltpu.VMEM),
        scratch_shapes=[
            pltpu.VMEM((16, chip_rows, depth), bf16),
            pltpu.VMEM((4, chip_rows, depth), bf16),
            pltpu.VMEM((2, 16, depth, each), bf16),
            pltpu.VMEM((2, chip_rows, each), f32),
            pltpu.VMEM((2, chip_rows, each), f32),
            pltpu.VMEM((2, chip_rows, each), f32),
            pltpu.VMEM((2, rows, each), f32),
            pltpu.VMEM((2, chip_rows, each), f32),
            pltpu.VMEM((2, rows, each), f32),
            pltpu.VMEM((2, rows, each), bf16),
            pltpu.VMEM((2, 8 * rows, each), bf16),
            pltpu.VMEM((8, rows), jnp.int32),
            pltpu.VMEM((8, 8 * rows), jnp.int32),
            pltpu.VMEM(w_up.shape, bf16),
            pltpu.VMEM(queries.shape[1:], bf16),
            pltpu.VMEM((KVH, QH // KVH * rows, 2 * HD), bf16),
            pltpu.VMEM((4, KVH, chip_rows, 2 * HD), bf16),
            pltpu.VMEM((4, KVH, chip_rows, 2 * HD), bf16),
            pltpu.VMEM((KVH, QH // KVH * rows, 2 * HD), f32),
            pltpu.VMEM((KVH, QH // KVH * rows, HD), f32),
            dma((16,)),
            dma((2,)),
            dma((16,)),
            dma((16,)),
            dma((8,)),
            dma((8,)),
            dma((160,)),
            dma((2, 16, 2)),
            dma((8,)),
            dma((8,)),
            dma((10,)),
            dma((10,)),
            dma((2, 11)),
            dma((2, 11)),
            dma((2,)),
        ],
        compiler_params=pltpu.CompilerParams(
            collective_id=0, has_side_effects=True, vmem_limit_bytes=50 * 2**20
        ),
        name="layer",
    )(*(pltpu.with_memory_space_constraint(a, pltpu.HBM) for a in (block_order, tokens, w_down, w_up, queries)))


def per_device(layers, plane, tokens, w_down, w_up, queries, block_order):
    local_rows = tokens.shape[1]
    half_rows = local_rows // 2
    if plane == 8 and layers == 4:
        return layer(tokens, w_down, w_up, queries, block_order)
    summed = jnp.dot(
        tokens[0],
        lax.all_gather(w_down, ("dp", "ctx"), axis=0, tiled=True),
        preferred_element_type=jnp.float32,
    )
    latent = lax.all_gather(summed.astype(jnp.bfloat16), "ctx", axis=0, tiled=True)
    order = lax.all_gather(block_order, "ctx", axis=1, tiled=True)
    positions = jnp.repeat(order, half_rows, axis=1) * half_rows + jnp.tile(
        jnp.arange(half_rows, dtype=jnp.int32), order.shape[1]
    )
    return attend(block_order, positions, latent, w_up, queries)


def solution(mesh):
    placed = (
        P("dp", "ctx", None),
        P(("dp", "ctx"), None),
        P(),
        P("dp", "ctx", None),
        P("dp", "ctx"),
    )
    sizes = mesh.shape["dp"], mesh.shape["ctx"]
    return jax.shard_map(
        functools.partial(per_device, *sizes), mesh=mesh, in_specs=placed, out_specs=P("dp", "ctx", None), check_vma=False
    )
```
